32 devices in a mesh: groups: 2 (over y), seq: 4 (over z), tp: 4 (over x, core).
Axes of the slice: x: 2, y: 2, z: 4, core: 2. Of those that a mesh axis runs over, the one named last changes fastest.
Arguments:
- query: bfloat16 [4096, 2048], P(('groups', 'seq'), 'tp'), parts along dimension 0, may hold values from -64 to 64
- key_head_rows: bfloat16 [4096, 512], P(('groups', 'seq'), 'tp'), parts along dimension 0, may hold values from -64 to 64
- value_head_rows: bfloat16 [4096, 512], P(('groups', 'seq'), 'tp'), parts along dimension 0, may hold values from -6 to 6
- output_gradient: bfloat16 [4096, 2048], P(('groups', 'seq'), 'tp'), parts along dimension 0, may hold values from -16 to 16
- doc_blocks: int32 [32, 8], P(('groups', 'seq')), parts along dimension 0, may hold values from 0 to 13, as said below
- w_query: bfloat16 [4096, 2048], P(None, 'tp'), may hold values from -0.5 to 0.5
- key_weight: bfloat16 [4096, 512], P(None, 'tp'), may hold values from -0.5 to 0.5
- value_weight: bfloat16 [4096, 512], P(None, 'tp'), may hold values from -0.5 to 0.5
Outputs:
- input_grad: bfloat16 [4096, 4096], P(('groups', 'seq'), 'tp'), parts along dimension 0
The draws below stay inside these ranges and needn't reach their ends.
There are 2 independent parts, one for each index of `groups`. The reference program is written for one: setup_inputs(seed, part) draws one part's arguments, and reference() takes and returns one part's arrays. A program takes and returns all parts, laid end to end along the dimension named above; an argument that names none is the same for every part. Nothing has to cross between parts.
Inputs may be any that keep to these rules, and one draw needn't show every extreme that they name: `doc_blocks`: row b holds max(b - o, 0) for 8 distinct offsets o of 2 to 12; every row b that starts a shard of 512 positions uses the offset 12, and the last row uses the offset 2.
All inputs are finite; a program needn't handle non-finite values.
Results may differ from the reference program's by a relative error of at most 0.014.
Values may be sent and summed in bfloat16 or wider, within the bound.
A program may use at most 128 MiB of HBM per device.

```python
import jax
import jax.numpy as jnp
from jax import lax

MODEL_WIDTH = 4096
QUERY_HEADS = 16
KEY_VALUE_HEADS = 4
HEAD_WIDTH = 128
BLOCK_POSITIONS = 128
LISTED_COUNT = 8
TOK_DEV = 512
TOKEN_COUNT = 2048
QUERY_BLOCK_COUNT = 16
SPAN_BLK = 12
N_TP = 4


def paired_rows(key):
    query_raw = jnp.clip(jax.random.normal(jax.random.fold_in(key, 11), (TOKEN_COUNT, QUERY_HEADS * HEAD_WIDTH), jnp.float32), -6.0, 6.0)
    key_unprojected = jnp.clip(jax.random.normal(jax.random.fold_in(key, 12), (TOKEN_COUNT, KEY_VALUE_HEADS * HEAD_WIDTH), jnp.float32), -6.0, 6.0)
    return (query_raw, key_unprojected)


def draw_query(key, part):
    return paired_rows(key)[0].astype(jnp.bfloat16)


def draw_key_head_rows(key, part):
    return paired_rows(key)[1].astype(jnp.bfloat16)


def draw_doc_blocks(key, part):
    option_count = SPAN_BLK - 1
    raw_scores = jax.random.randint(key, (QUERY_BLOCK_COUNT, option_count), 0, 1 << 20)
    sorted_scores = raw_scores * SPAN_BLK + jnp.arange(option_count)[None, :]
    row_index = jnp.arange(QUERY_BLOCK_COUNT)
    column_number = jnp.arange(option_count)[None, :]
    foremost_entries = row_index % (TOK_DEV // BLOCK_POSITIONS) == 0
    extra_score = jnp.where(foremost_entries[:, None] & (column_number == option_count - 1), 1 << 30, 0)
    closing_row = row_index == QUERY_BLOCK_COUNT - 1
    extra_score = extra_score + jnp.where(closing_row[:, None] & (column_number == 0), 1 << 30, 0)
    highest_values, selected_blocks = lax.top_k(sorted_scores + extra_score, LISTED_COUNT)
    block_ids = row_index[:, None] - (selected_blocks + 2)
    return jnp.maximum(block_ids, 0).astype(jnp.int32)


def level_of(key, extent, shards, smallest, largest):
    loudness = 1.0
    for dim, blocks in shards:
        steps = jax.random.uniform(jax.random.fold_in(jax.random.fold_in(key, 6), dim), (blocks,), jnp.float32, smallest / len(shards), largest / len(shards))
        loudness = loudness * jnp.repeat(jnp.exp(steps), extent[dim] // blocks).reshape((-1,) + (1,) * (len(extent) - 1 - dim))
    return loudness


def centred(own_key, shape, scale, limit, pieces=(), kind=jnp.bfloat16):
    level = level_of(own_key, shape, pieces, -0.22, 0.18) if pieces else 1.0
    result = jax.random.normal(own_key, shape, jnp.float32) * scale * level
    return jnp.minimum(jnp.maximum(result, -limit), limit).astype(kind)


def setup_inputs(seed: int = 0, part: int = 0) -> dict:
    splits = jax.random.split(jax.random.key(seed), 9)
    part_keys = jax.random.split(jax.random.fold_in(splits[8], part), 9)
    query = draw_query(jax.random.fold_in(jax.random.fold_in(splits[8], part), 71), part)
    key_head_rows = draw_key_head_rows(jax.random.fold_in(jax.random.fold_in(splits[8], part), 71), part)
    value_head_rows = centred(part_keys[2], (TOKEN_COUNT, KEY_VALUE_HEADS * HEAD_WIDTH), 1.0, 6.0, ((0, 4), (1, 4)))
    output_gradient = centred(part_keys[3], (TOKEN_COUNT, QUERY_HEADS * HEAD_WIDTH), 4.0, 16.0, ((0, 4), (1, 4)))
    doc_blocks = draw_doc_blocks(jax.random.fold_in(jax.random.fold_in(splits[8], part), 71), part)
    w_query = centred(splits[5], (MODEL_WIDTH, QUERY_HEADS * HEAD_WIDTH), HEAD_WIDTH ** -0.5, 0.5, ((1, 4),))
    key_weight = centred(splits[6], (MODEL_WIDTH, KEY_VALUE_HEADS * HEAD_WIDTH), HEAD_WIDTH ** -0.5, 0.5, ((1, 4),))
    value_weight = centred(splits[7], (MODEL_WIDTH, KEY_VALUE_HEADS * HEAD_WIDTH), HEAD_WIDTH ** -0.5, 0.5, ((1, 4),))
    return dict(query=query, key_head_rows=key_head_rows, value_head_rows=value_head_rows, output_gradient=output_gradient, doc_blocks=doc_blocks, w_query=w_query, key_weight=key_weight, value_weight=value_weight)


def block_grads(query_block, grad_block, key_block, value_block, allowed):
    score_scale = HEAD_WIDTH ** -0.5
    query_full = query_block.astype(jnp.float32)
    grad_full = grad_block.astype(jnp.float32)
    key_full = key_block.astype(jnp.float32)
    value_full = value_block.astype(jnp.float32)
    scores = jnp.einsum("qhgd,khd->hgqk", query_full, key_full) * score_scale
    scores = jnp.where(allowed, scores, -jnp.inf)
    row_max = jnp.max(scores, axis=-1, keepdims=True)
    weights = jnp.where(allowed, jnp.exp(scores - row_max), 0.0)
    probability = weights / jnp.sum(weights, axis=-1, keepdims=True)
    prob_half = lax.optimization_barrier(probability.astype(jnp.bfloat16)).astype(jnp.float32)
    attended = jnp.einsum("hgqk,khd->qhgd", prob_half, value_full)
    row_delta = jnp.sum(grad_full * attended, axis=-1)
    prob_grad = jnp.einsum("qhgd,khd->hgqk", grad_full, value_full)
    score_grad = probability * (prob_grad - jnp.transpose(row_delta, (1, 2, 0))[..., None])
    score_half = lax.optimization_barrier(score_grad.astype(jnp.bfloat16)).astype(jnp.float32)
    query_grad = jnp.einsum("hgqk,khd->qhgd", score_half, key_full) * score_scale
    key_gradient = jnp.einsum("hgqk,qhgd->khd", score_half, query_full) * score_scale
    value_gradient = jnp.einsum("hgqk,qhgd->khd", prob_half, grad_full)
    return query_grad, key_gradient, value_gradient


def reference(query, key_head_rows, value_head_rows, output_gradient, doc_blocks, w_query, key_weight, value_weight):
    group_width = QUERY_HEADS // KEY_VALUE_HEADS
    listed_slot_count = LISTED_COUNT + 2
    query_block_rows = query.reshape(QUERY_BLOCK_COUNT, BLOCK_POSITIONS, KEY_VALUE_HEADS, group_width, HEAD_WIDTH)
    gradient_blocks = output_gradient.reshape(QUERY_BLOCK_COUNT, BLOCK_POSITIONS, KEY_VALUE_HEADS, group_width, HEAD_WIDTH)
    key_block_rows = key_head_rows.reshape(QUERY_BLOCK_COUNT, BLOCK_POSITIONS, KEY_VALUE_HEADS, HEAD_WIDTH)
    value_block_rows = value_head_rows.reshape(QUERY_BLOCK_COUNT, BLOCK_POSITIONS, KEY_VALUE_HEADS, HEAD_WIDTH)
    offsets = jnp.arange(BLOCK_POSITIONS, dtype=jnp.int32)
    earlier = jnp.arange(LISTED_COUNT)[:, None] > jnp.arange(LISTED_COUNT)[None, :]
    far_slot = jnp.repeat(jnp.arange(listed_slot_count) >= 2, BLOCK_POSITIONS)

    def visit_block(sums_carry, block_id):
        key_gradient_sum, value_gradient_sum = sums_carry
        listed = doc_blocks[block_id].astype(jnp.int32)
        repeated = jnp.any((listed[:, None] == listed[None, :]) & earlier, axis=1)
        listed_ok = (listed <= block_id - 2) & jnp.logical_not(repeated)
        band_ids = jnp.stack([block_id - 1, block_id]).astype(jnp.int32)
        slot_ids = jnp.concatenate([band_ids, listed])
        slot_ok = jnp.concatenate([jnp.stack([block_id >= 1, block_id >= 0]), listed_ok])
        clamped_index = jnp.maximum(slot_ids, 0)
        query_pos = block_id * BLOCK_POSITIONS + offsets
        key_pos = (slot_ids[:, None] * BLOCK_POSITIONS + offsets[None, :]).reshape(-1)
        in_reach = (key_pos[None, :] <= query_pos[:, None]) & (query_pos[:, None] - key_pos[None, :] < BLOCK_POSITIONS)
        allowed = jnp.repeat(slot_ok, BLOCK_POSITIONS)[None, :] & (far_slot[None, :] | in_reach)
        present_keys = key_block_rows[clamped_index].reshape(listed_slot_count * BLOCK_POSITIONS, KEY_VALUE_HEADS, HEAD_WIDTH)
        present_values = value_block_rows[clamped_index].reshape(listed_slot_count * BLOCK_POSITIONS, KEY_VALUE_HEADS, HEAD_WIDTH)
        query_grad, key_gradient, value_gradient = block_grads(query_block_rows[block_id], gradient_blocks[block_id], present_keys, present_values, allowed)
        key_gradient_sum = key_gradient_sum.at[clamped_index].add(key_gradient.reshape(listed_slot_count, BLOCK_POSITIONS, KEY_VALUE_HEADS, HEAD_WIDTH))
        value_gradient_sum = value_gradient_sum.at[clamped_index].add(value_gradient.reshape(listed_slot_count, BLOCK_POSITIONS, KEY_VALUE_HEADS, HEAD_WIDTH))
        return (key_gradient_sum, value_gradient_sum), query_grad.astype(jnp.bfloat16)

    initial_zeros = jnp.zeros((QUERY_BLOCK_COUNT, BLOCK_POSITIONS, KEY_VALUE_HEADS, HEAD_WIDTH), jnp.float32)
    closing_sums, query_grads = lax.scan(visit_block, (initial_zeros, initial_zeros), jnp.arange(QUERY_BLOCK_COUNT, dtype=jnp.int32))
    query_grad_all = query_grads.reshape(TOKEN_COUNT, QUERY_HEADS * HEAD_WIDTH)
    key_gradient_total = closing_sums[0].reshape(TOKEN_COUNT, KEY_VALUE_HEADS * HEAD_WIDTH).astype(jnp.bfloat16)
    value_gradient_total = closing_sums[1].reshape(TOKEN_COUNT, KEY_VALUE_HEADS * HEAD_WIDTH).astype(jnp.bfloat16)
    query_cols = QUERY_HEADS * HEAD_WIDTH // N_TP
    key_value_columns = KEY_VALUE_HEADS * HEAD_WIDTH // N_TP
    summed = jnp.zeros((TOKEN_COUNT, MODEL_WIDTH), jnp.float32)
    for shard_index in range(N_TP):
        query_span = slice(shard_index * query_cols, (shard_index + 1) * query_cols)
        kv_span = slice(shard_index * key_value_columns, (shard_index + 1) * key_value_columns)
        grad_term = jnp.dot(query_grad_all[:, query_span], w_query[:, query_span].T, preferred_element_type=jnp.float32)
        grad_term = grad_term + jnp.dot(key_gradient_total[:, kv_span], key_weight[:, kv_span].T, preferred_element_type=jnp.float32)
        grad_term = grad_term + jnp.dot(value_gradient_total[:, kv_span], value_weight[:, kv_span].T, preferred_element_type=jnp.float32)
        summed = summed + lax.optimization_barrier(grad_term.astype(jnp.bfloat16)).astype(jnp.float32)
    return summed.astype(jnp.bfloat16)
```

```python
import functools

import jax
import jax.numpy as jnp
from jax import lax
from jax.experimental import pallas as pl
from jax.experimental.pallas import tpu as pltpu
from jax.sharding import PartitionSpec as P

HEAD_WIDTH = 128
BLOCK_POSITIONS = 128
MESH_ID = pl.DeviceIdType.MESH


def dot_t(a, b):
    return lax.dot_general(a, b, (((1,), (1,)), ((), ())), preferred_element_type=jnp.float32)


def dot_n(a, b):
    return lax.dot_general(a, b, (((1,), (0,)), ((), ())), preferred_element_type=jnp.float32)


def dot_lt(a, b):
    return lax.dot_general(a, b, (((0,), (0,)), ((), ())), preferred_element_type=jnp.float32)


def attention_kernel(
    shards,
    reach,
    q_ref,
    k_ref,
    v_ref,
    g_ref,
    docs_ref,
    dq_ref,
    dkv_ref,
    kv_win,
    q_heads,
    g_heads,
    stats,
    dq_sum,
    kv_sum,
    ret_out,
    ret_in,
    send_sem,
    recv_sem,
    ret_send,
    ret_recv,
):
    B = BLOCK_POSITIONS
    rows = k_ref.shape[0]
    nb = rows // B
    heads = q_ref.shape[1] // HEAD_WIDTH
    listed_count = docs_ref.shape[1]
    me = lax.axis_index("seq")
    scale = HEAD_WIDTH ** -0.5
    has_next = me + 1 < shards
    has_prev = me >= 1

    barrier = pltpu.get_barrier_semaphore()

    @pl.when(has_next)
    def _():
        pl.semaphore_signal(barrier, inc=1, device_id={"seq": me + 1}, device_id_type=MESH_ID)

    @pl.when(has_prev)
    def _():
        pl.semaphore_signal(barrier, inc=1, device_id={"seq": me - 1}, device_id_type=MESH_ID)

    pl.semaphore_wait(barrier, has_next.astype(jnp.int32) + has_prev.astype(jnp.int32))

    def forward(d, c):
        src = (k_ref, v_ref)[c] if d == 0 else kv_win.at[d - 1, c]
        return pltpu.make_async_remote_copy(
            src_ref=src,
            dst_ref=kv_win.at[d, c],
            send_sem=send_sem.at[d, c],
            recv_sem=recv_sem.at[d, c],
            device_id={"seq": jnp.minimum(me + 1, shards - 1)},
            device_id_type=MESH_ID,
        )

    def backward(d):
        return pltpu.make_async_remote_copy(
            src_ref=ret_out.at[d - 1],
            dst_ref=ret_in.at[d - 1],
            send_sem=ret_send.at[d - 1],
            recv_sem=ret_recv.at[d - 1],
            device_id={"seq": jnp.maximum(me - 1, 0)},
            device_id_type=MESH_ID,
        )

    @pl.when(has_next)
    def _():
        forward(0, 0).start()
        forward(0, 1).start()

    for i in range(nb):
        for h in range(heads):
            q_heads[i, h * B : (h + 1) * B, :] = q_ref[i * B : (i + 1) * B, h * HEAD_WIDTH : (h + 1) * HEAD_WIDTH]
            g_heads[i, h * B : (h + 1) * B, :] = g_ref[i * B : (i + 1) * B, h * HEAD_WIDTH : (h + 1) * HEAD_WIDTH]
    width = heads * B
    key_row = lax.broadcasted_iota(jnp.int32, (B, width), 0)
    query_row = lax.broadcasted_iota(jnp.int32, (B, width), 1) & (B - 1)
    own_mask = key_row <= query_row

    def keys_of(d):
        return (k_ref, v_ref) if d == 0 else (kv_win.at[d - 1, 0], kv_win.at[d - 1, 1])

    def masked_scores(d, i, j, raw):
        static = isinstance(i, int)
        offset = d * nb + i - j
        if static and offset == 0:
            return jnp.where(own_mask, raw * scale, -jnp.inf)
        if static and offset == 1:
            return jnp.where(own_mask, -jnp.inf, raw * scale)
        key_block = (me - d) * nb + j
        hits = jnp.int32(0)
        for n in range(listed_count):
            hits = hits | (docs_ref[i, n] == key_block).astype(jnp.int32)
        ok = (hits > 0) & (offset >= 2)
        bias = jnp.where(ok, jnp.float32(0.0), jnp.float32(-jnp.inf))
        return raw * scale + bias

    def stats_step(d, i):
        kref, vref = keys_of(d)
        last = i + 1 if d == 0 else nb
        q = q_heads[i]
        g = g_heads[i]
        raw = dot_t(kref[: last * B, :], q)
        s = jnp.concatenate(
            [masked_scores(d, i, j, raw[j * B : (j + 1) * B]) for j in range(last)], axis=0
        )
        prob_grad = dot_t(vref[: last * B, :], g)
        top = jnp.max(s, axis=0, keepdims=True)
        if d == 0:
            e = jnp.exp(s - top)
            stats[i, 0:1, :] = top
            stats[i, 1:2, :] = jnp.sum(e, axis=0, keepdims=True)
            stats[i, 2:3, :] = jnp.sum(e * prob_grad, axis=0, keepdims=True)
        else:
            old = stats[i, 0:1, :]
            new = jnp.maximum(old, top)
            keep = jnp.exp(old - new)
            e = jnp.exp(s - new)
            stats[i, 0:1, :] = new
            stats[i, 1:2, :] = stats[i, 1:2, :] * keep + jnp.sum(e, axis=0, keepdims=True)
            stats[i, 2:3, :] = stats[i, 2:3, :] * keep + jnp.sum(e * prob_grad, axis=0, keepdims=True)

    def grad_step(d, i, fresh):
        kref, vref = keys_of(d)
        last = i + 1 if d == 0 else nb
        q = q_heads[i]
        g = g_heads[i]
        keys = kref[: last * B, :]
        raw = dot_t(keys, q)
        s = jnp.concatenate(
            [masked_scores(d, i, j, raw[j * B : (j + 1) * B]) for j in range(last)], axis=0
        )
        prob_grad = dot_t(vref[: last * B, :], g)
        prob = jnp.exp(s - stats[i, 0:1, :]) * stats[i, 1:2, :]
        score_half = (prob * (prob_grad - stats[i, 2:3, :])).astype(jnp.bfloat16)
        prob_half = prob.astype(jnp.bfloat16)
        key_term = dot_n(score_half, q)
        value_term = dot_n(prob_half, g)
        if fresh:
            kv_sum[d, 0, : last * B, :] = key_term
            kv_sum[d, 1, : last * B, :] = value_term
        else:
            kv_sum[d, 0, : last * B, :] += key_term
            kv_sum[d, 1, : last * B, :] += value_term
        dq_sum[i] += dot_lt(keys, score_half)

    def over_blocks(d, step):
        if d == 0:
            for i in range(nb - 1, -1, -1):
                step(i, i == nb - 1)
            return
        step(0, True)

        def one(i, carry):
            step(i, False)
            return carry

        lax.fori_loop(1, nb, one, 0)

    for d in range(reach + 1):
        if d == 0:
            over_blocks(d, lambda i, fresh: stats_step(0, i))
            continue

        @pl.when(me >= d)
        def _():
            for c in range(2):
                forward(d - 1, c).wait_recv()

        if d < reach:

            @pl.when((me >= d) & has_next)
            def _():
                for c in range(2):
                    forward(d, c).start()

        @pl.when(me >= d)
        def _():
            over_blocks(d, lambda i, fresh: stats_step(d, i))

    for i in range(nb):
        inverse = 1.0 / stats[i, 1:2, :]
        stats[i, 1:2, :] = inverse
        stats[i, 2:3, :] = stats[i, 2:3, :] * inverse
        dq_sum[i] = jnp.zeros((HEAD_WIDTH, width), jnp.float32)

    def scaled(d, c):
        return kv_sum[d, c] * scale if c == 0 else kv_sum[d, c]

    for d in range(reach, -1, -1):

        @pl.when(me >= d)
        def _():
            over_blocks(d, lambda i, fresh: grad_step(d, i, fresh))

        if d == 0:
            continue
        first = me >= d if d == reach else (me >= d) & jnp.logical_not(has_next)

        @pl.when(first)
        def _():
            for c in range(2):
                ret_out[d - 1, c] = scaled(d, c).astype(jnp.bfloat16)
            backward(d).start()

    for i in range(nb):
        turned = (dq_sum[i] * scale).T.astype(jnp.bfloat16)
        for h in range(heads):
            dq_ref[i * B : (i + 1) * B, h * HEAD_WIDTH : (h + 1) * HEAD_WIDTH] = turned[h * B : (h + 1) * B]

    for d in range(reach - 1, 0, -1):

        @pl.when((me >= d) & has_next)
        def _():
            backward(d + 1).wait_recv()
            for c in range(2):
                ret_out[d - 1, c] = (scaled(d, c) + ret_in[d, c].astype(jnp.float32)).astype(jnp.bfloat16)
            backward(d).start()

    @pl.when(has_next)
    def _():
        backward(1).wait_recv()
        for c in range(2):
            dkv_ref[:, c * HEAD_WIDTH : (c + 1) * HEAD_WIDTH] = (
                scaled(0, c) + ret_in[0, c].astype(jnp.float32)
            ).astype(jnp.bfloat16)

    @pl.when(jnp.logical_not(has_next))
    def _():
        for c in range(2):
            dkv_ref[:, c * HEAD_WIDTH : (c + 1) * HEAD_WIDTH] = scaled(0, c).astype(jnp.bfloat16)

    for d in range(reach):

        @pl.when((me >= d) & has_next)
        def _():
            for c in range(2):
                forward(d, c).wait_send()

        @pl.when(me >= d + 1)
        def _():
            backward(d + 1).wait_send()


def attention(query, key_head_rows, value_head_rows, output_gradient, doc_blocks):
    shards = lax.axis_size("seq")
    reach = min(8, shards - 1)
    rows, q_width = query.shape
    nb = rows // BLOCK_POSITIONS
    width = (q_width // HEAD_WIDTH) * BLOCK_POSITIONS
    vmem = pl.BlockSpec(memory_space=pltpu.VMEM)
    return pl.pallas_call(
        functools.partial(attention_kernel, shards, reach),
        out_shape=[
            jax.ShapeDtypeStruct((rows, q_width), jnp.bfloat16),
            jax.ShapeDtypeStruct((rows, 2 * HEAD_WIDTH), jnp.bfloat16),
        ],
        in_specs=[vmem] * 4 + [pl.BlockSpec(memory_space=pltpu.SMEM)],
        out_specs=[vmem, vmem],
        scratch_shapes=[
            pltpu.VMEM((reach, 2, rows, HEAD_WIDTH), jnp.bfloat16),
            pltpu.VMEM((nb, width, HEAD_WIDTH), jnp.bfloat16),
            pltpu.VMEM((nb, width, HEAD_WIDTH), jnp.bfloat16),
            pltpu.VMEM((nb, 8, width), jnp.float32),
            pltpu.VMEM((nb, HEAD_WIDTH, width), jnp.float32),
            pltpu.VMEM((reach + 1, 2, rows, HEAD_WIDTH), jnp.float32),
            pltpu.VMEM((reach, 2, rows, HEAD_WIDTH), jnp.bfloat16),
            pltpu.VMEM((reach, 2, rows, HEAD_WIDTH), jnp.bfloat16),
            pltpu.SemaphoreType.DMA((reach, 2)),
            pltpu.SemaphoreType.DMA((reach, 2)),
            pltpu.SemaphoreType.DMA((reach,)),
            pltpu.SemaphoreType.DMA((reach,)),
        ],
        compiler_params=pltpu.CompilerParams(
            collective_id=0, has_side_effects=True, vmem_limit_bytes=60 * 1024 * 1024
        ),
        name="attention",
    )(query, key_head_rows, value_head_rows, output_gradient, doc_blocks)


def body(
    query,
    key_head_rows,
    value_head_rows,
    output_gradient,
    doc_blocks,
    w_query,
    key_weight,
    value_weight,
):
    query_sum, key_value_sum = attention(
        query, key_head_rows, value_head_rows, output_gradient, doc_blocks
    )
    contract = (((1,), (1,)), ((), ()))
    grad_term = lax.dot_general(query_sum, w_query, contract, preferred_element_type=jnp.float32)
    grad_term = grad_term + lax.dot_general(
        key_value_sum[:, :HEAD_WIDTH], key_weight, contract, preferred_element_type=jnp.float32
    )
    grad_term = grad_term + lax.dot_general(
        key_value_sum[:, HEAD_WIDTH:], value_weight, contract, preferred_element_type=jnp.float32
    )
    return lax.psum_scatter(
        grad_term.astype(jnp.bfloat16), "tp", scatter_dimension=1, tiled=True
    )


def solution(mesh):
    in_specs = (
        P(("groups", "seq"), "tp"),
        P(("groups", "seq"), "tp"),
        P(("groups", "seq"), "tp"),
        P(("groups", "seq"), "tp"),
        P(("groups", "seq"), None),
        P(None, "tp"),
        P(None, "tp"),
        P(None, "tp"),
    )
    out_specs = P(("groups", "seq"), "tp")
    return jax.shard_map(body, mesh=mesh, in_specs=in_specs, out_specs=out_specs, check_vma=False)
```

```python
import functools

import jax
import jax.numpy as jnp
from jax import lax
from jax.experimental import pallas as pl
from jax.experimental.pallas import tpu as pltpu
from jax.sharding import PartitionSpec as P

HEAD_WIDTH = 128
BLOCK_POSITIONS = 128
MESH_ID = pl.DeviceIdType.MESH


def dot_t(a, b):
    return lax.dot_general(a, b, (((1,), (1,)), ((), ())), preferred_element_type=jnp.float32)


def dot_n(a, b):
    return lax.dot_general(a, b, (((1,), (0,)), ((), ())), preferred_element_type=jnp.float32)


def dot_lt(a, b):
    return lax.dot_general(a, b, (((0,), (0,)), ((), ())), preferred_element_type=jnp.float32)


def attention_kernel(
    shards,
    reach,
    places,
    q_ref,
    k_ref,
    v_ref,
    g_ref,
    docs_ref,
    wq_hbm,
    wk_hbm,
    wv_hbm,
    out_ref,
    dq_ref,
    dkv_ref,
    wq_ref,
    wk_ref,
    wv_ref,
    near_sum,
    pair_out,
    pair_in,
    far_out,
    far_in,
    weight_sem,
    pair_send,
    pair_recv,
    far_send,
    far_recv,
    kv_win,
    q_heads,
    g_heads,
    stats,
    dq_sum,
    kv_sum,
    ret_out,
    ret_in,
    send_sem,
    recv_sem,
    ret_send,
    ret_recv,
):
    B = BLOCK_POSITIONS
    rows = k_ref.shape[0]
    nb = rows // B
    heads = q_ref.shape[1] // HEAD_WIDTH
    listed_count = docs_ref.shape[1]
    me = lax.axis_index("seq")
    scale = HEAD_WIDTH ** -0.5
    has_next = me + 1 < shards
    has_prev = me >= 1

    pairs = places // 2
    place = lax.axis_index("tp")
    my_pair = place // 2
    parity = place % 2
    partner = my_pair * 2 + 1 - parity
    cols = out_ref.shape[1]

    def peer_of(k):
        return lax.rem(my_pair + k, pairs) * 2 + parity

    def owner_of(k, mine):
        return lax.rem(my_pair + k, pairs) * 2 + (parity if mine else 1 - parity)

    barrier = pltpu.get_barrier_semaphore()
    pl.semaphore_signal(barrier, inc=1, device_id={"tp": partner}, device_id_type=MESH_ID)
    for k in range(1, pairs):
        pl.semaphore_signal(barrier, inc=1, device_id={"tp": peer_of(k)}, device_id_type=MESH_ID)

    @pl.when(has_next)
    def _():
        pl.semaphore_signal(barrier, inc=1, device_id={"seq": me + 1}, device_id_type=MESH_ID)

    @pl.when(has_prev)
    def _():
        pl.semaphore_signal(barrier, inc=1, device_id={"seq": me - 1}, device_id_type=MESH_ID)

    pl.semaphore_wait(barrier, has_next.astype(jnp.int32) + has_prev.astype(jnp.int32) + pairs)

    whole = [
        pltpu.make_async_copy(wq_hbm, wq_ref, weight_sem.at[0]),
        pltpu.make_async_copy(wk_hbm, wk_ref, weight_sem.at[1]),
        pltpu.make_async_copy(wv_hbm, wv_ref, weight_sem.at[2]),
    ]
    for copy in whole:
        copy.start()

    def forward(d, c):
        src = (k_ref, v_ref)[c] if d == 0 else kv_win.at[d - 1, c]
        return pltpu.make_async_remote_copy(
            src_ref=src,
            dst_ref=kv_win.at[d, c],
            send_sem=send_sem.at[d, c],
            recv_sem=recv_sem.at[d, c],
            device_id={"seq": jnp.minimum(me + 1, shards - 1)},
            device_id_type=MESH_ID,
        )

    def backward(d):
        return pltpu.make_async_remote_copy(
            src_ref=ret_out.at[d - 1],
            dst_ref=ret_in.at[d - 1],
            send_sem=ret_send.at[d - 1],
            recv_sem=ret_recv.at[d - 1],
            device_id={"seq": jnp.maximum(me - 1, 0)},
            device_id_type=MESH_ID,
        )

    @pl.when(has_next)
    def _():
        forward(0, 0).start()
        forward(0, 1).start()

    for i in range(nb):
        for h in range(heads):
            q_heads[i, h * B : (h + 1) * B, :] = q_ref[i * B : (i + 1) * B, h * HEAD_WIDTH : (h + 1) * HEAD_WIDTH]
            g_heads[i, h * B : (h + 1) * B, :] = g_ref[i * B : (i + 1) * B, h * HEAD_WIDTH : (h + 1) * HEAD_WIDTH]
    width = heads * B
    key_row = lax.broadcasted_iota(jnp.int32, (B, width), 0)
    query_row = lax.broadcasted_iota(jnp.int32, (B, width), 1) & (B - 1)
    own_mask = key_row <= query_row

    def keys_of(d):
        return (k_ref, v_ref) if d == 0 else (kv_win.at[d - 1, 0], kv_win.at[d - 1, 1])

    def masked_scores(d, i, j, raw):
        static = isinstance(i, int)
        offset = d * nb + i - j
        if static and offset == 0:
            return jnp.where(own_mask, raw * scale, -jnp.inf)
        if static and offset == 1:
            return jnp.where(own_mask, -jnp.inf, raw * scale)
        key_block = (me - d) * nb + j
        hits = jnp.int32(0)
        for n in range(listed_count):
            hits = hits | (docs_ref[i, n] == key_block).astype(jnp.int32)
        ok = (hits > 0) & (offset >= 2)
        bias = jnp.where(ok, jnp.float32(0.0), jnp.float32(-jnp.inf))
        return raw * scale + bias

    def stats_step(d, i):
        kref, vref = keys_of(d)
        last = i + 1 if d == 0 else nb
        q = q_heads[i]
        g = g_heads[i]
        raw = dot_t(kref[: last * B, :], q)
        s = jnp.concatenate(
            [masked_scores(d, i, j, raw[j * B : (j + 1) * B]) for j in range(last)], axis=0
        )
        prob_grad = dot_t(vref[: last * B, :], g)
        top = jnp.max(s, axis=0, keepdims=True)
        if d == 0:
            e = jnp.exp(s - top)
            stats[i, 0:1, :] = top
            stats[i, 1:2, :] = jnp.sum(e, axis=0, keepdims=True)
            stats[i, 2:3, :] = jnp.sum(e * prob_grad, axis=0, keepdims=True)
        else:
            old = stats[i, 0:1, :]
            new = jnp.maximum(old, top)
            keep = jnp.exp(old - new)
            e = jnp.exp(s - new)
            stats[i, 0:1, :] = new
            stats[i, 1:2, :] = stats[i, 1:2, :] * keep + jnp.sum(e, axis=0, keepdims=True)
            stats[i, 2:3, :] = stats[i, 2:3, :] * keep + jnp.sum(e * prob_grad, axis=0, keepdims=True)

    def grad_step(d, i, fresh):
        kref, vref = keys_of(d)
        last = i + 1 if d == 0 else nb
        q = q_heads[i]
        g = g_heads[i]
        keys = kref[: last * B, :]
        raw = dot_t(keys, q)
        s = jnp.concatenate(
            [masked_scores(d, i, j, raw[j * B : (j + 1) * B]) for j in range(last)], axis=0
        )
        prob_grad = dot_t(vref[: last * B, :], g)
        prob = jnp.exp(s - stats[i, 0:1, :]) * stats[i, 1:2, :]
        score_half = (prob * (prob_grad - stats[i, 2:3, :])).astype(jnp.bfloat16)
        prob_half = prob.astype(jnp.bfloat16)
        key_term = dot_n(score_half, q)
        value_term = dot_n(prob_half, g)
        if fresh:
            kv_sum[d, 0, : last * B, :] = key_term
            kv_sum[d, 1, : last * B, :] = value_term
        else:
            kv_sum[d, 0, : last * B, :] += key_term
            kv_sum[d, 1, : last * B, :] += value_term
        dq_sum[i] += dot_lt(keys, score_half)

    def over_blocks(d, step):
        if d == 0:
            for i in range(nb - 1, -1, -1):
                step(i, i == nb - 1)
            return
        step(0, True)

        def one(i, carry):
            step(i, False)
            return carry

        lax.fori_loop(1, nb, one, 0)

    for d in range(reach + 1):
        if d == 0:
            over_blocks(d, lambda i, fresh: stats_step(0, i))
            continue

        @pl.when(me >= d)
        def _():
            for c in range(2):
                forward(d - 1, c).wait_recv()

        if d < reach:

            @pl.when((me >= d) & has_next)
            def _():
                for c in range(2):
                    forward(d, c).start()

        @pl.when(me >= d)
        def _():
            over_blocks(d, lambda i, fresh: stats_step(d, i))

    for i in range(nb):
        inverse = 1.0 / stats[i, 1:2, :]
        stats[i, 1:2, :] = inverse
        stats[i, 2:3, :] = stats[i, 2:3, :] * inverse
        dq_sum[i] = jnp.zeros((HEAD_WIDTH, width), jnp.float32)

    def scaled(d, c):
        return kv_sum[d, c] * scale if c == 0 else kv_sum[d, c]

    for d in range(reach, -1, -1):

        @pl.when(me >= d)
        def _():
            over_blocks(d, lambda i, fresh: grad_step(d, i, fresh))

        if d == 0:
            continue
        first = me >= d if d == reach else (me >= d) & jnp.logical_not(has_next)

        @pl.when(first)
        def _():
            for c in range(2):
                ret_out[d - 1, c] = scaled(d, c).astype(jnp.bfloat16)
            backward(d).start()

    for i in range(nb):
        turned = (dq_sum[i] * scale).T.astype(jnp.bfloat16)
        for h in range(heads):
            dq_ref[i * B : (i + 1) * B, h * HEAD_WIDTH : (h + 1) * HEAD_WIDTH] = turned[h * B : (h + 1) * B]

    for d in range(reach - 1, 0, -1):

        @pl.when((me >= d) & has_next)
        def _():
            backward(d + 1).wait_recv()
            for c in range(2):
                ret_out[d - 1, c] = (scaled(d, c) + ret_in[d, c].astype(jnp.float32)).astype(jnp.bfloat16)
            backward(d).start()

    @pl.when(has_next)
    def _():
        backward(1).wait_recv()
        for c in range(2):
            dkv_ref[:, c * HEAD_WIDTH : (c + 1) * HEAD_WIDTH] = (
                scaled(0, c) + ret_in[0, c].astype(jnp.float32)
            ).astype(jnp.bfloat16)

    @pl.when(jnp.logical_not(has_next))
    def _():
        for c in range(2):
            dkv_ref[:, c * HEAD_WIDTH : (c + 1) * HEAD_WIDTH] = scaled(0, c).astype(jnp.bfloat16)

    chunks = nb
    step_rows = rows // chunks
    for copy in whole:
        copy.wait()

    def term(owner, c):
        span = pl.ds(pl.multiple_of(owner * cols, cols), cols)
        part = slice(c * step_rows, (c + 1) * step_rows)
        value = dot_t(dq_ref[part, :], wq_ref[span, :])
        value = value + dot_t(dkv_ref[part, :HEAD_WIDTH], wk_ref[span, :])
        return value + dot_t(dkv_ref[part, HEAD_WIDTH:], wv_ref[span, :])

    def to_pair(k, c):
        return pltpu.make_async_remote_copy(
            src_ref=pair_out.at[k, c],
            dst_ref=pair_in.at[k, c],
            send_sem=pair_send.at[k, c],
            recv_sem=pair_recv.at[k, c],
            device_id={"tp": partner},
            device_id_type=MESH_ID,
        )

    def to_far(k, c):
        return pltpu.make_async_remote_copy(
            src_ref=far_out.at[k - 1, c],
            dst_ref=far_in.at[k - 1, c],
            send_sem=far_send.at[k - 1, c],
            recv_sem=far_recv.at[k - 1, c],
            device_id={"tp": peer_of(k)},
            device_id_type=MESH_ID,
        )

    def give(k, c):
        pair_out[k, c] = term(owner_of(k, False), c).astype(jnp.bfloat16)
        to_pair(k, c).start()

    def take(k, c):
        value = term(owner_of(k, True), c)
        to_pair(k, c).wait_recv()
        value = value + pair_in[k, c].astype(jnp.float32)
        if k == 0:
            near_sum[c] = value
        else:
            far_out[k - 1, c] = value.astype(jnp.bfloat16)
            to_far(k, c).start()

    order = [(k, c) for k in list(range(1, pairs)) + [0] for c in range(chunks)]
    give(*order[0])
    for n, item in enumerate(order):
        if n + 1 < len(order):
            give(*order[n + 1])
        take(*item)
    for c in range(chunks):
        value = near_sum[c]
        for k in range(1, pairs):
            to_far(k, c).wait_recv()
            value = value + far_in[k - 1, c].astype(jnp.float32)
        out_ref[c * step_rows : (c + 1) * step_rows, :] = value.astype(jnp.bfloat16)
    for k, c in order:
        to_pair(k, c).wait_send()
        if k > 0:
            to_far(k, c).wait_send()

    for d in range(reach):

        @pl.when((me >= d) & has_next)
        def _():
            for c in range(2):
                forward(d, c).wait_send()

        @pl.when(me >= d + 1)
        def _():
            backward(d + 1).wait_send()


def body(
    query,
    key_head_rows,
    value_head_rows,
    output_gradient,
    doc_blocks,
    w_query,
    key_weight,
    value_weight,
):
    shards = lax.axis_size("seq")
    places = lax.axis_size("tp")
    pairs = places // 2
    reach = min(8, shards - 1)
    rows, q_width = query.shape
    nb = rows // BLOCK_POSITIONS
    cols = w_query.shape[0] // places
    width = (q_width // HEAD_WIDTH) * BLOCK_POSITIONS
    half, full = jnp.bfloat16, jnp.float32
    vmem = pl.BlockSpec(memory_space=pltpu.VMEM)
    anywhere = pl.BlockSpec(memory_space=pl.ANY)
    dma = pltpu.SemaphoreType.DMA
    return pl.pallas_call(
        functools.partial(attention_kernel, shards, reach, places),
        out_shape=jax.ShapeDtypeStruct((rows, cols), half),
        in_specs=[vmem] * 4 + [pl.BlockSpec(memory_space=pltpu.SMEM)] + [anywhere] * 3,
        out_specs=vmem,
        scratch_shapes=[
            pltpu.VMEM((rows, q_width), half),
            pltpu.VMEM((rows, 2 * HEAD_WIDTH), half),
            pltpu.VMEM(w_query.shape, half),
            pltpu.VMEM(key_weight.shape, half),
            pltpu.VMEM(value_weight.shape, half),
            pltpu.VMEM((nb, rows // nb, cols), full),
            pltpu.VMEM((pairs, nb, rows // nb, cols), half),
            pltpu.VMEM((pairs, nb, rows // nb, cols), half),
            pltpu.VMEM((pairs - 1, nb, rows // nb, cols), half),
            pltpu.VMEM((pairs - 1, nb, rows // nb, cols), half),
            dma((3,)),
            dma((pairs, nb)),
            dma((pairs, nb)),
            dma((pairs - 1, nb)),
            dma((pairs - 1, nb)),
            pltpu.VMEM((reach, 2, rows, HEAD_WIDTH), half),
            pltpu.VMEM((nb, width, HEAD_WIDTH), half),
            pltpu.VMEM((nb, width, HEAD_WIDTH), half),
            pltpu.VMEM((nb, 8, width), full),
            pltpu.VMEM((nb, HEAD_WIDTH, width), full),
            pltpu.VMEM((reach + 1, 2, rows, HEAD_WIDTH), full),
            pltpu.VMEM((reach, 2, rows, HEAD_WIDTH), half),
            pltpu.VMEM((reach, 2, rows, HEAD_WIDTH), half),
            dma((reach, 2)),
            dma((reach, 2)),
            dma((reach,)),
            dma((reach,)),
        ],
        compiler_params=pltpu.CompilerParams(
            collective_id=0, has_side_effects=True, vmem_limit_bytes=60 * 1024 * 1024
        ),
        name="attention",
    )(
        query,
        key_head_rows,
        value_head_rows,
        output_gradient,
        doc_blocks,
        w_query,
        key_weight,
        value_weight,
    )


def solution(mesh):
    in_specs = (
        P(("groups", "seq"), "tp"),
        P(("groups", "seq"), "tp"),
        P(("groups", "seq"), "tp"),
        P(("groups", "seq"), "tp"),
        P(("groups", "seq"), None),
        P(None, "tp"),
        P(None, "tp"),
        P(None, "tp"),
    )
    out_specs = P(("groups", "seq"), "tp")
    return jax.shard_map(body, mesh=mesh, in_specs=in_specs, out_specs=out_specs, check_vma=False)
```

```python
import functools
import math

import jax
import jax.numpy as jnp
from jax import lax
from jax.experimental import pallas as pl
from jax.experimental.pallas import tpu as pltpu
from jax.sharding import PartitionSpec as P

HEAD_WIDTH = 128
BLOCK_POSITIONS = 128
MESH_ID = pl.DeviceIdType.MESH


def dot_t(a, b):
    return lax.dot_general(a, b, (((1,), (1,)), ((), ())), preferred_element_type=jnp.float32)


def dot_n(a, b):
    return lax.dot_general(a, b, (((1,), (0,)), ((), ())), preferred_element_type=jnp.float32)


def dot_lt(a, b):
    return lax.dot_general(a, b, (((0,), (0,)), ((), ())), preferred_element_type=jnp.float32)


def attention_kernel(
    shards,
    reach,
    places,
    q_ref,
    k_ref,
    v_ref,
    g_ref,
    docs_ref,
    wq_hbm,
    wk_hbm,
    wv_hbm,
    out_ref,
    dq_ref,
    dkv_ref,
    wq_ref,
    wk_ref,
    wv_ref,
    near_sum,
    pair_out,
    pair_in,
    far_out,
    far_in,
    weight_sem,
    pair_send,
    pair_recv,
    far_send,
    far_recv,
    kv_win,
    q_heads,
    g_heads,
    stats,
    dq_sum,
    probs,
    kv_sum,
    ret_out,
    ret_in,
    send_sem,
    recv_sem,
    ret_send,
    ret_recv,
):
    B = BLOCK_POSITIONS
    rows = k_ref.shape[0]
    nb = rows // B
    heads = q_ref.shape[1] // HEAD_WIDTH
    listed_count = docs_ref.shape[1]
    me = lax.axis_index("seq")
    scale = HEAD_WIDTH ** -0.5
    scale2 = scale * math.log2(math.e)
    has_next = me + 1 < shards
    has_prev = me >= 1

    pairs = places // 2
    place = lax.axis_index("tp")
    my_pair = place // 2
    parity = place % 2
    partner = my_pair * 2 + 1 - parity
    cols = out_ref.shape[1]

    def peer_of(k):
        return lax.rem(my_pair + k, pairs) * 2 + parity

    def owner_of(k, mine):
        return lax.rem(my_pair + k, pairs) * 2 + (parity if mine else 1 - parity)

    barrier = pltpu.get_barrier_semaphore()
    pl.semaphore_signal(barrier, inc=1, device_id={"tp": partner}, device_id_type=MESH_ID)
    for k in range(1, pairs):
        pl.semaphore_signal(barrier, inc=1, device_id={"tp": peer_of(k)}, device_id_type=MESH_ID)

    @pl.when(has_next)
    def _():
        pl.semaphore_signal(barrier, inc=1, device_id={"seq": me + 1}, device_id_type=MESH_ID)

    @pl.when(has_prev)
    def _():
        pl.semaphore_signal(barrier, inc=1, device_id={"seq": me - 1}, device_id_type=MESH_ID)

    pl.semaphore_wait(barrier, has_next.astype(jnp.int32) + has_prev.astype(jnp.int32) + pairs)

    whole = [
        pltpu.make_async_copy(wq_hbm, wq_ref, weight_sem.at[0]),
        pltpu.make_async_copy(wk_hbm, wk_ref, weight_sem.at[1]),
        pltpu.make_async_copy(wv_hbm, wv_ref, weight_sem.at[2]),
    ]
    for copy in whole:
        copy.start()

    def forward(d, c):
        src = (k_ref, v_ref)[c] if d == 0 else kv_win.at[d - 1, c]
        return pltpu.make_async_remote_copy(
            src_ref=src,
            dst_ref=kv_win.at[d, c],
            send_sem=send_sem.at[d, c],
            recv_sem=recv_sem.at[d, c],
            device_id={"seq": jnp.minimum(me + 1, shards - 1)},
            device_id_type=MESH_ID,
        )

    def backward(d, c):
        return pltpu.make_async_remote_copy(
            src_ref=ret_out.at[d - 1, c],
            dst_ref=ret_in.at[d - 1, c],
            send_sem=ret_send.at[d - 1, c],
            recv_sem=ret_recv.at[d - 1, c],
            device_id={"seq": jnp.maximum(me - 1, 0)},
            device_id_type=MESH_ID,
        )

    @pl.when(has_next)
    def _():
        forward(0, 0).start()

    for i in range(nb):
        for h in range(heads):
            q_heads[i, h * B : (h + 1) * B, :] = q_ref[i * B : (i + 1) * B, h * HEAD_WIDTH : (h + 1) * HEAD_WIDTH]
            g_heads[i, h * B : (h + 1) * B, :] = g_ref[i * B : (i + 1) * B, h * HEAD_WIDTH : (h + 1) * HEAD_WIDTH]
    width = heads * B
    key_row = lax.broadcasted_iota(jnp.int32, (B, width), 0)
    query_row = lax.broadcasted_iota(jnp.int32, (B, width), 1) & (B - 1)
    own_mask = key_row <= query_row

    def keys_of(d):
        return (k_ref, v_ref) if d == 0 else (kv_win.at[d - 1, 0], kv_win.at[d - 1, 1])

    def key_span(d, i):
        if isinstance(i, int) and d == 0:
            return 0, i + 1
        if isinstance(i, int) and d == reach:
            return i, nb
        return 0, nb

    def biased(d, i, j, raw):
        offset = d * nb + i - j
        if isinstance(i, int) and offset == 0:
            return jnp.where(own_mask, raw, -jnp.inf), jnp.float32(0.0)
        if isinstance(i, int) and offset == 1:
            return jnp.where(own_mask, -jnp.inf, raw), jnp.float32(0.0)
        key_block = (me - d) * nb + j
        hits = jnp.int32(0)
        for n in range(listed_count):
            hits = hits | (docs_ref[i, n] == key_block).astype(jnp.int32)
        ok = (hits > 0) & (offset >= 2)
        return raw, jnp.where(ok, jnp.float32(0.0), jnp.float32(-jnp.inf))

    def raw_blocks(d, i):
        low, high = key_span(d, i)
        raw = dot_t(keys_of(d)[0][low * B : high * B, :], q_heads[i])
        return [
            biased(d, i, j, raw[(j - low) * B : (j - low + 1) * B]) for j in range(low, high)
        ]

    def stats_step(d, i, fresh):
        blocks = raw_blocks(d, i)
        tops = [jnp.max(raw, axis=0, keepdims=True) * scale2 + bias for raw, bias in blocks]
        new = functools.reduce(jnp.maximum, tops)
        if d > 0:
            old = stats[i, 0:1, :]
            new = jnp.maximum(old, new)
        total = 0.0
        for raw, bias in blocks:
            total = total + jnp.sum(jnp.exp2(raw * scale2 + (bias - new)), axis=0, keepdims=True)
        if d > 0:
            total = total + stats[i, 1:2, :] * jnp.exp2(old - new)
        stats[i, 0:1, :] = new
        stats[i, 1:2, :] = total

    def value_step(d, i, fresh):
        low, high = key_span(d, i)
        top = stats[i, 0:1, :]
        inverse = stats[i, 1:2, :]
        parts = [
            (jnp.exp2(raw * scale2 + (bias - top)) * inverse).astype(jnp.bfloat16)
            for raw, bias in raw_blocks(d, i)
        ]
        prob_half = jnp.concatenate(parts, axis=0)
        probs[d, i, low * B : high * B, :] = prob_half
        term = dot_n(prob_half, g_heads[i])
        if fresh:
            kv_sum[d, 1, low * B : high * B, :] = term
        else:
            kv_sum[d, 1, low * B : high * B, :] += term

    def delta_step(d, i, fresh):
        low, high = key_span(d, i)
        prob_grad = dot_t(keys_of(d)[1][low * B : high * B, :], g_heads[i])
        prob = probs[d, i, low * B : high * B, :].astype(jnp.float32)
        stats[i, 2:3, :] += jnp.sum(prob * prob_grad, axis=0, keepdims=True)

    def grad_step(d, i, fresh):
        low, high = key_span(d, i)
        keys = keys_of(d)[0][low * B : high * B, :]
        prob_grad = dot_t(keys_of(d)[1][low * B : high * B, :], g_heads[i])
        prob = probs[d, i, low * B : high * B, :].astype(jnp.float32)
        score_half = (prob * (prob_grad - stats[i, 2:3, :])).astype(jnp.bfloat16)
        term = dot_n(score_half, q_heads[i])
        if fresh:
            kv_sum[d, 0, low * B : high * B, :] = term
        else:
            kv_sum[d, 0, low * B : high * B, :] += term
        dq_sum[i] += dot_lt(keys, score_half)

    def over_blocks(d, step):
        if d == 0:
            for i in range(nb - 1, -1, -1):
                step(d, i, i == nb - 1)
            return
        step(d, 0, True)
        if d == reach:
            for i in range(1, nb):
                step(d, i, False)
            return

        def one(i, carry):
            step(d, i, False)
            return carry

        lax.fori_loop(1, nb, one, 0)

    def present(d, step):
        @pl.when(me >= d)
        def _():
            over_blocks(d, step)

    def arrive(d, c):
        @pl.when(me >= d)
        def _():
            forward(d - 1, c).wait_recv()

        if d < reach:

            @pl.when((me >= d) & has_next)
            def _():
                forward(d, c).start()

    def start_values():
        @pl.when(has_next)
        def _():
            forward(0, 1).start()

    def scaled(d, c):
        return kv_sum[d, c] * scale if c == 0 else kv_sum[d, c]

    def send_first(d, c):
        first = me >= d if d == reach else (me >= d) & jnp.logical_not(has_next)

        @pl.when(first)
        def _():
            ret_out[d - 1, c] = scaled(d, c).astype(jnp.bfloat16)
            backward(d, c).start()

    def send_on(d, c):
        @pl.when((me >= d) & has_next)
        def _():
            backward(d + 1, c).wait_recv()
            ret_out[d - 1, c] = (scaled(d, c) + ret_in[d, c].astype(jnp.float32)).astype(jnp.bfloat16)
            backward(d, c).start()

    for d in range(reach + 1):
        if d > 0:
            arrive(d, 0)
        if d == reach - 1:
            start_values()
        present(d, stats_step)

    for i in range(nb):
        stats[i, 1:2, :] = 1.0 / stats[i, 1:2, :]
        stats[i, 2:3, :] = jnp.zeros((1, width), jnp.float32)
        dq_sum[i] = jnp.zeros((HEAD_WIDTH, width), jnp.float32)

    for n in range(1, reach):
        present(reach - n + 1, value_step)
        send_first(reach - n + 1, 1)
        arrive(n, 1)
    present(1, value_step)
    send_first(1, 1)
    present(0, value_step)
    for d in range(reach):
        present(d, delta_step)
    arrive(reach, 1)
    present(reach, delta_step)

    for d in range(reach, -1, -1):
        if d >= 2:
            send_on(d - 1, 1)
        present(d, grad_step)
        if d >= 1:
            send_first(d, 0)

    for i in range(nb):
        turned = (dq_sum[i] * scale).T.astype(jnp.bfloat16)
        for h in range(heads):
            dq_ref[i * B : (i + 1) * B, h * HEAD_WIDTH : (h + 1) * HEAD_WIDTH] = turned[h * B : (h + 1) * B]

    for d in range(reach - 1, 0, -1):
        send_on(d, 0)

    @pl.when(has_next)
    def _():
        for c in (1, 0):
            backward(1, c).wait_recv()
            dkv_ref[:, c * HEAD_WIDTH : (c + 1) * HEAD_WIDTH] = (
                scaled(0, c) + ret_in[0, c].astype(jnp.float32)
            ).astype(jnp.bfloat16)

    @pl.when(jnp.logical_not(has_next))
    def _():
        for c in range(2):
            dkv_ref[:, c * HEAD_WIDTH : (c + 1) * HEAD_WIDTH] = scaled(0, c).astype(jnp.bfloat16)

    chunks = nb
    step_rows = rows // chunks
    for copy in whole:
        copy.wait()

    def term(owner, c):
        span = pl.ds(pl.multiple_of(owner * cols, cols), cols)
        part = slice(c * step_rows, (c + 1) * step_rows)
        value = dot_t(dq_ref[part, :], wq_ref[span, :])
        value = value + dot_t(dkv_ref[part, :HEAD_WIDTH], wk_ref[span, :])
        return value + dot_t(dkv_ref[part, HEAD_WIDTH:], wv_ref[span, :])

    def to_pair(k, c):
        return pltpu.make_async_remote_copy(
            src_ref=pair_out.at[k, c],
            dst_ref=pair_in.at[k, c],
            send_sem=pair_send.at[k, c],
            recv_sem=pair_recv.at[k, c],
            device_id={"tp": partner},
            device_id_type=MESH_ID,
        )

    def to_far(k, c):
        return pltpu.make_async_remote_copy(
            src_ref=far_out.at[k - 1, c],
            dst_ref=far_in.at[k - 1, c],
            send_sem=far_send.at[k - 1, c],
            recv_sem=far_recv.at[k - 1, c],
            device_id={"tp": peer_of(k)},
            device_id_type=MESH_ID,
        )

    def give(k, c):
        pair_out[k, c] = term(owner_of(k, False), c).astype(jnp.bfloat16)
        to_pair(k, c).start()

    def take(k, c):
        value = term(owner_of(k, True), c)
        to_pair(k, c).wait_recv()
        value = value + pair_in[k, c].astype(jnp.float32)
        if k == 0:
            near_sum[c] = value
        else:
            far_out[k - 1, c] = value.astype(jnp.bfloat16)
            to_far(k, c).start()

    order = [(k, c) for k in list(range(1, pairs)) + [0] for c in range(chunks)]
    give(*order[0])
    for n, item in enumerate(order):
        if n + 1 < len(order):
            give(*order[n + 1])
        take(*item)
    for c in range(chunks):
        value = near_sum[c]
        for k in range(1, pairs):
            to_far(k, c).wait_recv()
            value = value + far_in[k - 1, c].astype(jnp.float32)
        out_ref[c * step_rows : (c + 1) * step_rows, :] = value.astype(jnp.bfloat16)
    for k, c in order:
        to_pair(k, c).wait_send()
        if k > 0:
            to_far(k, c).wait_send()

    for d in range(reach):

        @pl.when((me >= d) & has_next)
        def _():
            for c in range(2):
                forward(d, c).wait_send()

        @pl.when(me >= d + 1)
        def _():
            for c in range(2):
                backward(d + 1, c).wait_send()


def body(
    query,
    key_head_rows,
    value_head_rows,
    output_gradient,
    doc_blocks,
    w_query,
    key_weight,
    value_weight,
):
    shards = lax.axis_size("seq")
    places = lax.axis_size("tp")
    pairs = places // 2
    reach = min(8, shards - 1)
    rows, q_width = query.shape
    nb = rows // BLOCK_POSITIONS
    cols = w_query.shape[0] // places
    width = (q_width // HEAD_WIDTH) * BLOCK_POSITIONS
    half, full = jnp.bfloat16, jnp.float32
    vmem = pl.BlockSpec(memory_space=pltpu.VMEM)
    anywhere = pl.BlockSpec(memory_space=pl.ANY)
    dma = pltpu.SemaphoreType.DMA
    return pl.pallas_call(
        functools.partial(attention_kernel, shards, reach, places),
        out_shape=jax.ShapeDtypeStruct((rows, cols), half),
        in_specs=[vmem] * 4 + [pl.BlockSpec(memory_space=pltpu.SMEM)] + [anywhere] * 3,
        out_specs=vmem,
        scratch_shapes=[
            pltpu.VMEM((rows, q_width), half),
            pltpu.VMEM((rows, 2 * HEAD_WIDTH), half),
            pltpu.VMEM(w_query.shape, half),
            pltpu.VMEM(key_weight.shape, half),
            pltpu.VMEM(value_weight.shape, half),
            pltpu.VMEM((nb, rows // nb, cols), full),
            pltpu.VMEM((pairs, nb, rows // nb, cols), half),
            pltpu.VMEM((pairs, nb, rows // nb, cols), half),
            pltpu.VMEM((pairs - 1, nb, rows // nb, cols), half),
            pltpu.VMEM((pairs - 1, nb, rows // nb, cols), half),
            dma((3,)),
            dma((pairs, nb)),
            dma((pairs, nb)),
            dma((pairs - 1, nb)),
            dma((pairs - 1, nb)),
            pltpu.VMEM((reach, 2, rows, HEAD_WIDTH), half),
            pltpu.VMEM((nb, width, HEAD_WIDTH), half),
            pltpu.VMEM((nb, width, HEAD_WIDTH), half),
            pltpu.VMEM((nb, 8, width), full),
            pltpu.VMEM((nb, HEAD_WIDTH, width), full),
            pltpu.VMEM((reach + 1, nb, rows, width), half),
            pltpu.VMEM((reach + 1, 2, rows, HEAD_WIDTH), full),
            pltpu.VMEM((reach, 2, rows, HEAD_WIDTH), half),
            pltpu.VMEM((reach, 2, rows, HEAD_WIDTH), half),
            dma((reach, 2)),
            dma((reach, 2)),
            dma((reach, 2)),
            dma((reach, 2)),
        ],
        compiler_params=pltpu.CompilerParams(
            collective_id=0, has_side_effects=True, vmem_limit_bytes=60 * 1024 * 1024
        ),
        name="attention",
    )(
        query,
        key_head_rows,
        value_head_rows,
        output_gradient,
        doc_blocks,
        w_query,
        key_weight,
        value_weight,
    )


def solution(mesh):
    in_specs = (
        P(("groups", "seq"), "tp"),
        P(("groups", "seq"), "tp"),
        P(("groups", "seq"), "tp"),
        P(("groups", "seq"), "tp"),
        P(("groups", "seq"), None),
        P(None, "tp"),
        P(None, "tp"),
        P(None, "tp"),
    )
    out_specs = P(("groups", "seq"), "tp")
    return jax.shard_map(body, mesh=mesh, in_specs=in_specs, out_specs=out_specs, check_vma=False)
```

```python
import functools
import math

import jax
import jax.numpy as jnp
from jax import lax
from jax.experimental import pallas as pl
from jax.experimental.pallas import tpu as pltpu
from jax.sharding import PartitionSpec as P

HEAD_WIDTH = 128
BLOCK_POSITIONS = 128
MESH_ID = pl.DeviceIdType.MESH


def dot_t(a, b):
    return lax.dot_general(a, b, (((1,), (1,)), ((), ())), preferred_element_type=jnp.float32)


def dot_n(a, b):
    return lax.dot_general(a, b, (((1,), (0,)), ((), ())), preferred_element_type=jnp.float32)


def dot_lt(a, b):
    return lax.dot_general(a, b, (((0,), (0,)), ((), ())), preferred_element_type=jnp.float32)


def attention_kernel(
    shards,
    reach,
    places,
    q_ref,
    k_ref,
    v_ref,
    g_ref,
    docs_ref,
    wq_hbm,
    wk_hbm,
    wv_hbm,
    out_ref,
    dq_ref,
    dkv_ref,
    dkv_now,
    dkv_all,
    wk_all,
    wv_all,
    wq_ref,
    wk_ref,
    wv_ref,
    near_sum,
    pair_out,
    pair_in,
    far_out,
    far_in,
    weight_sem,
    pair_send,
    pair_recv,
    far_send,
    far_recv,
    fetch_send,
    fetch_recv,
    gather_send,
    gather_recv,
    kv_win,
    q_heads,
    g_heads,
    stats,
    dq_sum,
    probs,
    kv_sum,
    ret_out,
    ret_in,
    send_sem,
    recv_sem,
    ret_send,
    ret_recv,
):
    B = BLOCK_POSITIONS
    rows = k_ref.shape[0]
    nb = rows // B
    heads = q_ref.shape[1] // HEAD_WIDTH
    listed_count = docs_ref.shape[1]
    me = lax.axis_index("seq")
    scale = HEAD_WIDTH ** -0.5
    scale2 = scale * math.log2(math.e)
    has_next = me + 1 < shards
    has_prev = me >= 1

    pairs = places // 2
    place = lax.axis_index("tp")
    my_pair = place // 2
    parity = place % 2
    partner = my_pair * 2 + 1 - parity
    cols = out_ref.shape[1]

    def peer_of(k):
        return lax.rem(my_pair + k, pairs) * 2 + parity

    def owner_of(k, mine):
        return lax.rem(my_pair + k, pairs) * 2 + (parity if mine else 1 - parity)

    barrier = pltpu.get_barrier_semaphore()
    others = [(k, m) for k in range(pairs) for m in range(2) if (k, m) != (0, 0)]
    for k, m in others:
        pl.semaphore_signal(barrier, inc=1, device_id={"tp": owner_of(k, m == 0)}, device_id_type=MESH_ID)

    @pl.when(has_next)
    def _():
        pl.semaphore_signal(barrier, inc=1, device_id={"seq": me + 1}, device_id_type=MESH_ID)

    @pl.when(has_prev)
    def _():
        pl.semaphore_signal(barrier, inc=1, device_id={"seq": me - 1}, device_id_type=MESH_ID)

    pl.semaphore_wait(barrier, has_next.astype(jnp.int32) + has_prev.astype(jnp.int32) + places - 1)

    whole = [
        pltpu.make_async_copy(wq_hbm, wq_ref, weight_sem.at[0]),
        pltpu.make_async_copy(wk_hbm, wk_ref, weight_sem.at[1]),
        pltpu.make_async_copy(wv_hbm, wv_ref, weight_sem.at[2]),
    ]
    for copy in whole:
        copy.start()

    def forward(d, c):
        src = (k_ref, v_ref)[c] if d == 0 else kv_win.at[d - 1, c]
        return pltpu.make_async_remote_copy(
            src_ref=src,
            dst_ref=kv_win.at[d, c],
            send_sem=send_sem.at[d, c],
            recv_sem=recv_sem.at[d, c],
            device_id={"seq": jnp.minimum(me + 1, shards - 1)},
            device_id_type=MESH_ID,
        )

    def backward(d, c):
        return pltpu.make_async_remote_copy(
            src_ref=ret_out.at[d - 1, c],
            dst_ref=ret_in.at[d - 1, c],
            send_sem=ret_send.at[d - 1, c],
            recv_sem=ret_recv.at[d - 1, c],
            device_id={"seq": jnp.maximum(me - 1, 0)},
            device_id_type=MESH_ID,
        )

    @pl.when(has_next)
    def _():
        forward(0, 0).start()

    for i in range(nb):
        for h in range(heads):
            q_heads[i, h * B : (h + 1) * B, :] = q_ref[i * B : (i + 1) * B, h * HEAD_WIDTH : (h + 1) * HEAD_WIDTH]
            g_heads[i, h * B : (h + 1) * B, :] = g_ref[i * B : (i + 1) * B, h * HEAD_WIDTH : (h + 1) * HEAD_WIDTH]
    width = heads * B
    key_row = lax.broadcasted_iota(jnp.int32, (B, width), 0)
    query_row = lax.broadcasted_iota(jnp.int32, (B, width), 1) & (B - 1)
    own_mask = key_row <= query_row

    def span_of(owner):
        return pl.ds(pl.multiple_of(owner * cols, cols), cols)

    def fetch(k, m, c):
        owner = owner_of(k, m == 0)
        return pltpu.make_async_remote_copy(
            src_ref=(wk_hbm, wv_hbm)[c].at[span_of(owner)],
            dst_ref=(wk_all, wv_all)[c].at[k, m],
            send_sem=fetch_send.at[k, m, c],
            recv_sem=fetch_recv.at[k, m, c],
            device_id={"tp": owner},
            device_id_type=MESH_ID,
        )

    def gather(k, m):
        return pltpu.make_async_remote_copy(
            src_ref=dkv_all.at[k, 0] if m == 1 and k > 0 else dkv_ref,
            dst_ref=dkv_all.at[k, m],
            send_sem=gather_send.at[k, m],
            recv_sem=gather_recv.at[k, m],
            device_id={"tp": partner if m == 1 else peer_of(k)},
            device_id_type=MESH_ID,
        )

    @pl.when(has_next)
    def _():
        for k, m in others:
            for c in range(2):
                fetch(k, m, c).start()

    def keys_of(d):
        return (k_ref, v_ref) if d == 0 else (kv_win.at[d - 1, 0], kv_win.at[d - 1, 1])

    def key_span(d, i):
        if isinstance(i, int) and d == 0:
            return 0, i + 1
        if isinstance(i, int) and d == reach:
            return i, nb
        return 0, nb

    def biased(d, i, j, raw):
        offset = d * nb + i - j
        if isinstance(i, int) and offset == 0:
            return jnp.where(own_mask, raw, -jnp.inf), jnp.float32(0.0)
        if isinstance(i, int) and offset == 1:
            return jnp.where(own_mask, -jnp.inf, raw), jnp.float32(0.0)
        key_block = (me - d) * nb + j
        hits = jnp.int32(0)
        for n in range(listed_count):
            hits = hits | (docs_ref[i, n] == key_block).astype(jnp.int32)
        ok = (hits > 0) & (offset >= 2)
        return raw, jnp.where(ok, jnp.float32(0.0), jnp.float32(-jnp.inf))

    def raw_blocks(d, i):
        low, high = key_span(d, i)
        raw = dot_t(keys_of(d)[0][low * B : high * B, :], q_heads[i])
        return [
            biased(d, i, j, raw[(j - low) * B : (j - low + 1) * B]) for j in range(low, high)
        ]

    def stats_step(d, i, fresh):
        blocks = raw_blocks(d, i)
        tops = [jnp.max(raw, axis=0, keepdims=True) * scale2 + bias for raw, bias in blocks]
        new = functools.reduce(jnp.maximum, tops)
        if d > 0:
            old = stats[i, 0:1, :]
            new = jnp.maximum(old, new)
        total = 0.0
        for raw, bias in blocks:
            total = total + jnp.sum(jnp.exp2(raw * scale2 + (bias - new)), axis=0, keepdims=True)
        if d > 0:
            total = total + stats[i, 1:2, :] * jnp.exp2(old - new)
        stats[i, 0:1, :] = new
        stats[i, 1:2, :] = total

    def value_step(d, i, fresh):
        low, high = key_span(d, i)
        top = stats[i, 0:1, :]
        inverse = stats[i, 1:2, :]
        parts = [
            (jnp.exp2(raw * scale2 + (bias - top)) * inverse).astype(jnp.bfloat16)
            for raw, bias in raw_blocks(d, i)
        ]
        prob_half = jnp.concatenate(parts, axis=0)
        probs[d, i, low * B : high * B, :] = prob_half
        term = dot_n(prob_half, g_heads[i])
        if fresh:
            kv_sum[d, 1, low * B : high * B, :] = term
        else:
            kv_sum[d, 1, low * B : high * B, :] += term

    def delta_step(d, i, fresh):
        low, high = key_span(d, i)
        prob_grad = dot_t(keys_of(d)[1][low * B : high * B, :], g_heads[i])
        prob = probs[d, i, low * B : high * B, :].astype(jnp.float32)
        stats[i, 2:3, :] += jnp.sum(prob * prob_grad, axis=0, keepdims=True)

    def grad_step(d, i, fresh):
        low, high = key_span(d, i)
        keys = keys_of(d)[0][low * B : high * B, :]
        prob_grad = dot_t(keys_of(d)[1][low * B : high * B, :], g_heads[i])
        prob = probs[d, i, low * B : high * B, :].astype(jnp.float32)
        score_half = (prob * (prob_grad - stats[i, 2:3, :])).astype(jnp.bfloat16)
        term = dot_n(score_half, q_heads[i])
        if fresh:
            kv_sum[d, 0, low * B : high * B, :] = term
        else:
            kv_sum[d, 0, low * B : high * B, :] += term
        dq_sum[i] += dot_lt(keys, score_half)

    def over_blocks(d, step):
        if d == 0:
            for i in range(nb - 1, -1, -1):
                step(d, i, i == nb - 1)
            return
        step(d, 0, True)
        if d == reach:
            for i in range(1, nb):
                step(d, i, False)
            return

        def one(i, carry):
            step(d, i, False)
            return carry

        lax.fori_loop(1, nb, one, 0)

    def present(d, step):
        @pl.when(me >= d)
        def _():
            over_blocks(d, step)

    def arrive(d, c):
        @pl.when(me >= d)
        def _():
            forward(d - 1, c).wait_recv()

        if d < reach:

            @pl.when((me >= d) & has_next)
            def _():
                forward(d, c).start()

    def start_values():
        @pl.when(has_next)
        def _():
            forward(0, 1).start()

    def scaled(d, c):
        return kv_sum[d, c] * scale if c == 0 else kv_sum[d, c]

    def send_first(d, c):
        first = me >= d if d == reach else (me >= d) & jnp.logical_not(has_next)

        @pl.when(first)
        def _():
            ret_out[d - 1, c] = scaled(d, c).astype(jnp.bfloat16)
            backward(d, c).start()

    def send_on(d, c):
        @pl.when((me >= d) & has_next)
        def _():
            backward(d + 1, c).wait_recv()
            ret_out[d - 1, c] = (scaled(d, c) + ret_in[d, c].astype(jnp.float32)).astype(jnp.bfloat16)
            backward(d, c).start()

    for d in range(reach + 1):
        if d > 0:
            arrive(d, 0)
        if d == reach - 1:
            start_values()
        present(d, stats_step)

    for i in range(nb):
        stats[i, 1:2, :] = 1.0 / stats[i, 1:2, :]
        stats[i, 2:3, :] = jnp.zeros((1, width), jnp.float32)
        dq_sum[i] = jnp.zeros((HEAD_WIDTH, width), jnp.float32)

    for n in range(1, reach):
        present(reach - n + 1, value_step)
        send_first(reach - n + 1, 1)
        arrive(n, 1)
    present(1, value_step)
    send_first(1, 1)
    present(0, value_step)
    for d in range(reach):
        present(d, delta_step)
    arrive(reach, 1)
    present(reach, delta_step)

    for d in range(reach, -1, -1):
        if d >= 2:
            send_on(d - 1, 1)
        present(d, grad_step)
        if d >= 1:
            send_first(d, 0)

    for i in range(nb):
        turned = (dq_sum[i] * scale).T.astype(jnp.bfloat16)
        for h in range(heads):
            dq_ref[i * B : (i + 1) * B, h * HEAD_WIDTH : (h + 1) * HEAD_WIDTH] = turned[h * B : (h + 1) * B]

    for c in range(2):
        dkv_now[:, c * HEAD_WIDTH : (c + 1) * HEAD_WIDTH] = jnp.where(
            has_next, jnp.float32(0.0), scaled(0, c)
        ).astype(jnp.bfloat16)

    chunks = nb
    step_rows = rows // chunks
    for copy in whole:
        copy.wait()

    def term(owner, c):
        span = pl.ds(pl.multiple_of(owner * cols, cols), cols)
        part = slice(c * step_rows, (c + 1) * step_rows)
        value = dot_t(dq_ref[part, :], wq_ref[span, :])
        value = value + dot_t(dkv_now[part, :HEAD_WIDTH], wk_ref[span, :])
        return value + dot_t(dkv_now[part, HEAD_WIDTH:], wv_ref[span, :])

    def to_pair(k, c):
        return pltpu.make_async_remote_copy(
            src_ref=pair_out.at[k, c],
            dst_ref=pair_in.at[k, c],
            send_sem=pair_send.at[k, c],
            recv_sem=pair_recv.at[k, c],
            device_id={"tp": partner},
            device_id_type=MESH_ID,
        )

    def to_far(k, c):
        return pltpu.make_async_remote_copy(
            src_ref=far_out.at[k - 1, c],
            dst_ref=far_in.at[k - 1, c],
            send_sem=far_send.at[k - 1, c],
            recv_sem=far_recv.at[k - 1, c],
            device_id={"tp": peer_of(k)},
            device_id_type=MESH_ID,
        )

    def give(k, c):
        pair_out[k, c] = term(owner_of(k, False), c).astype(jnp.bfloat16)
        to_pair(k, c).start()

    def take(k, c):
        value = term(owner_of(k, True), c)
        to_pair(k, c).wait_recv()
        value = value + pair_in[k, c].astype(jnp.float32)
        if k == 0:
            near_sum[c] = value
        else:
            far_out[k - 1, c] = value.astype(jnp.bfloat16)
            to_far(k, c).start()

    order = [(k, c) for k in list(range(1, pairs)) + [0] for c in range(chunks)]
    give(*order[0])
    for n, item in enumerate(order):
        if n + 1 < len(order):
            give(*order[n + 1])
        take(*item)
    for d in range(reach - 1, 0, -1):
        send_on(d, 0)

    @pl.when(has_next)
    def _():
        for c in (1, 0):
            backward(1, c).wait_recv()
            dkv_ref[:, c * HEAD_WIDTH : (c + 1) * HEAD_WIDTH] = (
                scaled(0, c) + ret_in[0, c].astype(jnp.float32)
            ).astype(jnp.bfloat16)
        gather(0, 1).start()
        for k in range(1, pairs):
            gather(k, 0).start()

    def add_terms(pairs_of):
        for c in range(chunks):
            part = slice(c * step_rows, (c + 1) * step_rows)
            value = near_sum[c]
            for grads, wk, wv in pairs_of:
                value = value + dot_t(grads[part, :HEAD_WIDTH], wk[...])
                value = value + dot_t(grads[part, HEAD_WIDTH:], wv[...])
            near_sum[c] = value

    @pl.when(has_next)
    def _():
        for k, m in others:
            for c in range(2):
                fetch(k, m, c).wait_recv()
        own = span_of(place)
        add_terms([(dkv_ref, wk_ref.at[own], wv_ref.at[own])])
        gather(0, 1).wait_recv()
        add_terms([(dkv_all.at[0, 1], wk_all.at[0, 1], wv_all.at[0, 1])])
        for k in range(1, pairs):
            gather(k, 0).wait_recv()
            gather(k, 1).start()
            add_terms([(dkv_all.at[k, 0], wk_all.at[k, 0], wv_all.at[k, 0])])
        for k in range(1, pairs):
            gather(k, 1).wait_recv()
            add_terms([(dkv_all.at[k, 1], wk_all.at[k, 1], wv_all.at[k, 1])])
        for k, m in others:
            gather(k, m).wait_send()
            for c in range(2):
                fetch(k, m, c).wait_send()

    for c in range(chunks):
        value = near_sum[c]
        for k in range(1, pairs):
            to_far(k, c).wait_recv()
            value = value + far_in[k - 1, c].astype(jnp.float32)
        out_ref[c * step_rows : (c + 1) * step_rows, :] = value.astype(jnp.bfloat16)
    for k, c in order:
        to_pair(k, c).wait_send()
        if k > 0:
            to_far(k, c).wait_send()

    for d in range(reach):

        @pl.when((me >= d) & has_next)
        def _():
            for c in range(2):
                forward(d, c).wait_send()

        @pl.when(me >= d + 1)
        def _():
            for c in range(2):
                backward(d + 1, c).wait_send()


def body(
    query,
    key_head_rows,
    value_head_rows,
    output_gradient,
    doc_blocks,
    w_query,
    key_weight,
    value_weight,
):
    shards = lax.axis_size("seq")
    places = lax.axis_size("tp")
    pairs = places // 2
    reach = min(8, shards - 1)
    rows, q_width = query.shape
    nb = rows // BLOCK_POSITIONS
    cols = w_query.shape[0] // places
    width = (q_width // HEAD_WIDTH) * BLOCK_POSITIONS
    half, full = jnp.bfloat16, jnp.float32
    vmem = pl.BlockSpec(memory_space=pltpu.VMEM)
    anywhere = pl.BlockSpec(memory_space=pl.ANY)
    dma = pltpu.SemaphoreType.DMA
    return pl.pallas_call(
        functools.partial(attention_kernel, shards, reach, places),
        out_shape=jax.ShapeDtypeStruct((rows, cols), half),
        in_specs=[vmem] * 4 + [pl.BlockSpec(memory_space=pltpu.SMEM)] + [anywhere] * 3,
        out_specs=vmem,
        scratch_shapes=[
            pltpu.VMEM((rows, q_width), half),
            pltpu.VMEM((rows, 2 * HEAD_WIDTH), half),
            pltpu.VMEM((rows, 2 * HEAD_WIDTH), half),
            pltpu.VMEM((pairs, 2, rows, 2 * HEAD_WIDTH), half),
            pltpu.VMEM((pairs, 2, cols, HEAD_WIDTH), half),
            pltpu.VMEM((pairs, 2, cols, HEAD_WIDTH), half),
            pltpu.VMEM(w_query.shape, half),
            pltpu.VMEM(key_weight.shape, half),
            pltpu.VMEM(value_weight.shape, half),
            pltpu.VMEM((nb, rows // nb, cols), full),
            pltpu.VMEM((pairs, nb, rows // nb, cols), half),
            pltpu.VMEM((pairs, nb, rows // nb, cols), half),
            pltpu.VMEM((pairs - 1, nb, rows // nb, cols), half),
            pltpu.VMEM((pairs - 1, nb, rows // nb, cols), half),
            dma((3,)),
            dma((pairs, nb)),
            dma((pairs, nb)),
            dma((pairs - 1, nb)),
            dma((pairs - 1, nb)),
            dma((pairs, 2, 2)),
            dma((pairs, 2, 2)),
            dma((pairs, 2)),
            dma((pairs, 2)),
            pltpu.VMEM((reach, 2, rows, HEAD_WIDTH), half),
            pltpu.VMEM((nb, width, HEAD_WIDTH), half),
            pltpu.VMEM((nb, width, HEAD_WIDTH), half),
            pltpu.VMEM((nb, 8, width), full),
            pltpu.VMEM((nb, HEAD_WIDTH, width), full),
            pltpu.VMEM((reach + 1, nb, rows, width), half),
            pltpu.VMEM((reach + 1, 2, rows, HEAD_WIDTH), full),
            pltpu.VMEM((reach, 2, rows, HEAD_WIDTH), half),
            pltpu.VMEM((reach, 2, rows, HEAD_WIDTH), half),
            dma((reach, 2)),
            dma((reach, 2)),
            dma((reach, 2)),
            dma((reach, 2)),
        ],
        compiler_params=pltpu.CompilerParams(
            collective_id=0, has_side_effects=True, vmem_limit_bytes=60 * 1024 * 1024
        ),
        name="attention",
    )(
        query,
        key_head_rows,
        value_head_rows,
        output_gradient,
        doc_blocks,
        w_query,
        key_weight,
        value_weight,
    )


def solution(mesh):
    in_specs = (
        P(("groups", "seq"), "tp"),
        P(("groups", "seq"), "tp"),
        P(("groups", "seq"), "tp"),
        P(("groups", "seq"), "tp"),
        P(("groups", "seq"), None),
        P(None, "tp"),
        P(None, "tp"),
        P(None, "tp"),
    )
    out_specs = P(("groups", "seq"), "tp")
    return jax.shard_map(body, mesh=mesh, in_specs=in_specs, out_specs=out_specs, check_vma=False)
```

```python
import functools
import math

import jax
import jax.numpy as jnp
from jax import lax
from jax.experimental import pallas as pl
from jax.experimental.pallas import tpu as pltpu
from jax.sharding import PartitionSpec as P

HEAD_WIDTH = 128
BLOCK_POSITIONS = 128
MESH_ID = pl.DeviceIdType.MESH


def dot_t(a, b):
    return lax.dot_general(a, b, (((1,), (1,)), ((), ())), preferred_element_type=jnp.float32)


def dot_n(a, b):
    return lax.dot_general(a, b, (((1,), (0,)), ((), ())), preferred_element_type=jnp.float32)


def dot_lt(a, b):
    return lax.dot_general(a, b, (((0,), (0,)), ((), ())), preferred_element_type=jnp.float32)


def attention_kernel(
    shards,
    reach,
    places,
    q_ref,
    k_ref,
    v_ref,
    g_ref,
    docs_ref,
    wq_hbm,
    wk_hbm,
    wv_hbm,
    out_ref,
    dq_ref,
    dkv_ref,
    dkv_now,
    dkv_all,
    wk_all,
    wv_all,
    wq_ref,
    wk_ref,
    wv_ref,
    near_sum,
    pair_out,
    pair_in,
    far_out,
    far_in,
    weight_sem,
    pair_send,
    pair_recv,
    far_send,
    far_recv,
    fetch_send,
    fetch_recv,
    gather_send,
    gather_recv,
    kv_win,
    q_heads,
    g_heads,
    stats,
    dq_sum,
    probs,
    kv_sum,
    ret_out,
    ret_in,
    send_sem,
    recv_sem,
    ret_send,
    ret_recv,
):
    B = BLOCK_POSITIONS
    rows = k_ref.shape[0]
    nb = rows // B
    heads = q_ref.shape[1] // HEAD_WIDTH
    listed_count = docs_ref.shape[1]
    me = lax.axis_index("seq")
    scale = HEAD_WIDTH ** -0.5
    scale2 = scale * math.log2(math.e)
    has_next = me + 1 < shards
    has_prev = me >= 1

    pairs = places // 2
    place = lax.axis_index("tp")
    my_pair = place // 2
    parity = place % 2
    partner = my_pair * 2 + 1 - parity
    cols = out_ref.shape[1]

    def peer_of(k):
        return lax.rem(my_pair + k, pairs) * 2 + parity

    def owner_of(k, mine):
        return lax.rem(my_pair + k, pairs) * 2 + (parity if mine else 1 - parity)

    barrier = pltpu.get_barrier_semaphore()
    others = [(k, m) for k in range(pairs) for m in range(2) if (k, m) != (0, 0)]
    for k, m in others:
        pl.semaphore_signal(barrier, inc=1, device_id={"tp": owner_of(k, m == 0)}, device_id_type=MESH_ID)

    @pl.when(has_next)
    def _():
        pl.semaphore_signal(barrier, inc=1, device_id={"seq": me + 1}, device_id_type=MESH_ID)

    @pl.when(has_prev)
    def _():
        pl.semaphore_signal(barrier, inc=1, device_id={"seq": me - 1}, device_id_type=MESH_ID)

    pl.semaphore_wait(barrier, has_next.astype(jnp.int32) + has_prev.astype(jnp.int32) + places - 1)

    whole = [
        pltpu.make_async_copy(wq_hbm, wq_ref, weight_sem.at[0]),
        pltpu.make_async_copy(wk_hbm, wk_ref, weight_sem.at[1]),
        pltpu.make_async_copy(wv_hbm, wv_ref, weight_sem.at[2]),
    ]
    for copy in whole:
        copy.start()

    def forward(d, c):
        src = (k_ref, v_ref)[c] if d == 0 else kv_win.at[d - 1, c]
        return pltpu.make_async_remote_copy(
            src_ref=src,
            dst_ref=kv_win.at[d, c],
            send_sem=send_sem.at[d, c],
            recv_sem=recv_sem.at[d, c],
            device_id={"seq": jnp.minimum(me + 1, shards - 1)},
            device_id_type=MESH_ID,
        )

    def backward(d, c):
        return pltpu.make_async_remote_copy(
            src_ref=ret_out.at[d - 1, c],
            dst_ref=ret_in.at[d - 1, c],
            send_sem=ret_send.at[d - 1, c],
            recv_sem=ret_recv.at[d - 1, c],
            device_id={"seq": jnp.maximum(me - 1, 0)},
            device_id_type=MESH_ID,
        )

    @pl.when(has_next)
    def _():
        forward(0, 0).start()

    for i in range(nb):
        for h in range(heads):
            q_heads[i, h * B : (h + 1) * B, :] = q_ref[i * B : (i + 1) * B, h * HEAD_WIDTH : (h + 1) * HEAD_WIDTH]
            g_heads[i, h * B : (h + 1) * B, :] = g_ref[i * B : (i + 1) * B, h * HEAD_WIDTH : (h + 1) * HEAD_WIDTH]
    width = heads * B
    key_row = lax.broadcasted_iota(jnp.int32, (B, width), 0)
    query_row = lax.broadcasted_iota(jnp.int32, (B, width), 1) & (B - 1)
    own_mask = key_row <= query_row

    def span_of(owner):
        return pl.ds(pl.multiple_of(owner * cols, cols), cols)

    def fetch(k, m, c):
        owner = owner_of(k, m == 0)
        return pltpu.make_async_remote_copy(
            src_ref=(wk_hbm, wv_hbm)[c].at[span_of(owner)],
            dst_ref=(wk_all, wv_all)[c].at[k, m],
            send_sem=fetch_send.at[k, m, c],
            recv_sem=fetch_recv.at[k, m, c],
            device_id={"tp": owner},
            device_id_type=MESH_ID,
        )

    def gather(k, m):
        return pltpu.make_async_remote_copy(
            src_ref=dkv_all.at[k, 0] if m == 1 and k > 0 else dkv_ref,
            dst_ref=dkv_all.at[k, m],
            send_sem=gather_send.at[k, m],
            recv_sem=gather_recv.at[k, m],
            device_id={"tp": partner if m == 1 else peer_of(k)},
            device_id_type=MESH_ID,
        )

    @pl.when(has_next)
    def _():
        for k, m in others:
            for c in range(2):
                fetch(k, m, c).start()

    def keys_of(d):
        return (k_ref, v_ref) if d == 0 else (kv_win.at[d - 1, 0], kv_win.at[d - 1, 1])

    def key_span(d, i):
        if isinstance(i, int) and d == 0:
            return 0, i + 1
        if isinstance(i, int) and d == reach:
            return i, nb
        return 0, nb

    def biased(d, i, j, raw):
        offset = d * nb + i - j
        if isinstance(i, int) and offset == 0:
            return jnp.where(own_mask, raw, -jnp.inf), jnp.float32(0.0)
        if isinstance(i, int) and offset == 1:
            return jnp.where(own_mask, -jnp.inf, raw), jnp.float32(0.0)
        key_block = (me - d) * nb + j
        hits = jnp.int32(0)
        for n in range(listed_count):
            hits = hits | (docs_ref[i, n] == key_block).astype(jnp.int32)
        ok = (hits > 0) & (offset >= 2)
        return raw, jnp.where(ok, jnp.float32(0.0), jnp.float32(-jnp.inf))

    def raw_blocks(d, i):
        low, high = key_span(d, i)
        raw = dot_t(keys_of(d)[0][low * B : high * B, :], q_heads[i])
        return [
            biased(d, i, j, raw[(j - low) * B : (j - low + 1) * B]) for j in range(low, high)
        ]

    def stats_step(d, i, fresh):
        blocks = raw_blocks(d, i)
        tops = [jnp.max(raw, axis=0, keepdims=True) * scale2 + bias for raw, bias in blocks]
        new = functools.reduce(jnp.maximum, tops)
        if d > 0:
            old = stats[i, 0:1, :]
            new = jnp.maximum(old, new)
        total = 0.0
        for raw, bias in blocks:
            total = total + jnp.sum(jnp.exp2(raw * scale2 + (bias - new)), axis=0, keepdims=True)
        if d > 0:
            total = total + stats[i, 1:2, :] * jnp.exp2(old - new)
        stats[i, 0:1, :] = new
        stats[i, 1:2, :] = total

    def value_step(d, i, fresh):
        low, high = key_span(d, i)
        top = stats[i, 0:1, :]
        inverse = stats[i, 1:2, :]
        parts = [
            (jnp.exp2(raw * scale2 + (bias - top)) * inverse).astype(jnp.bfloat16)
            for raw, bias in raw_blocks(d, i)
        ]
        prob_half = jnp.concatenate(parts, axis=0)
        probs[d, i, low * B : high * B, :] = prob_half
        term = dot_n(prob_half, g_heads[i])
        if fresh:
            kv_sum[d, 1, low * B : high * B, :] = term
        else:
            kv_sum[d, 1, low * B : high * B, :] += term

    def delta_step(d, i, fresh):
        low, high = key_span(d, i)
        prob_grad = dot_t(keys_of(d)[1][low * B : high * B, :], g_heads[i])
        prob = probs[d, i, low * B : high * B, :].astype(jnp.float32)
        stats[i, 2:3, :] += jnp.sum(prob * prob_grad, axis=0, keepdims=True)

    def grad_step(d, i, fresh):
        low, high = key_span(d, i)
        keys = keys_of(d)[0][low * B : high * B, :]
        prob_grad = dot_t(keys_of(d)[1][low * B : high * B, :], g_heads[i])
        prob = probs[d, i, low * B : high * B, :].astype(jnp.float32)
        score_half = (prob * (prob_grad - stats[i, 2:3, :])).astype(jnp.bfloat16)
        term = dot_n(score_half, q_heads[i])
        if fresh:
            kv_sum[d, 0, low * B : high * B, :] = term
        else:
            kv_sum[d, 0, low * B : high * B, :] += term
        dq_sum[i] += dot_lt(keys, score_half)

    def over_blocks(d, step):
        if d == 0:
            for i in range(nb - 1, -1, -1):
                step(d, i, i == nb - 1)
            return
        step(d, 0, True)
        if d == reach:
            for i in range(1, nb):
                step(d, i, False)
            return

        def one(i, carry):
            step(d, i, False)
            return carry

        lax.fori_loop(1, nb, one, 0)

    def present(d, step):
        @pl.when(me >= d)
        def _():
            over_blocks(d, step)

    def arrive(d, c):
        @pl.when(me >= d)
        def _():
            forward(d - 1, c).wait_recv()

        if d < reach:

            @pl.when((me >= d) & has_next)
            def _():
                forward(d, c).start()

    def start_values():
        @pl.when(has_next)
        def _():
            forward(0, 1).start()

    def scaled(d, c):
        return kv_sum[d, c] * scale if c == 0 else kv_sum[d, c]

    def send_first(d, c):
        first = me >= d if d == reach else (me >= d) & jnp.logical_not(has_next)

        @pl.when(first)
        def _():
            ret_out[d - 1, c] = scaled(d, c).astype(jnp.bfloat16)
            backward(d, c).start()

    def send_on(d, c):
        @pl.when((me >= d) & has_next)
        def _():
            backward(d + 1, c).wait_recv()
            ret_out[d - 1, c] = (scaled(d, c) + ret_in[d, c].astype(jnp.float32)).astype(jnp.bfloat16)
            backward(d, c).start()

    for d in range(reach + 1):
        if d > 0:
            arrive(d, 0)
        if d == reach - 1:
            start_values()
        present(d, stats_step)

    for i in range(nb):
        stats[i, 1:2, :] = 1.0 / stats[i, 1:2, :]
        stats[i, 2:3, :] = jnp.zeros((1, width), jnp.float32)
        dq_sum[i] = jnp.zeros((HEAD_WIDTH, width), jnp.float32)

    for n in range(1, reach):
        present(reach - n + 1, value_step)
        send_first(reach - n + 1, 1)
        arrive(n, 1)
    present(1, value_step)
    send_first(1, 1)
    present(0, value_step)
    for d in range(reach):
        present(d, delta_step)
    arrive(reach, 1)
    present(reach, delta_step)

    for d in range(reach, -1, -1):
        if d >= 2:
            send_on(d - 1, 1)
        present(d, grad_step)
        if d >= 1:
            send_first(d, 0)

    for i in range(nb):
        turned = (dq_sum[i] * scale).T.astype(jnp.bfloat16)
        for h in range(heads):
            dq_ref[i * B : (i + 1) * B, h * HEAD_WIDTH : (h + 1) * HEAD_WIDTH] = turned[h * B : (h + 1) * B]

    for c in range(2):
        dkv_now[:, c * HEAD_WIDTH : (c + 1) * HEAD_WIDTH] = jnp.where(
            has_next, jnp.float32(0.0), scaled(0, c)
        ).astype(jnp.bfloat16)

    chunks = nb
    step_rows = rows // chunks
    for copy in whole:
        copy.wait()

    def term(owner, c):
        span = pl.ds(pl.multiple_of(owner * cols, cols), cols)
        part = slice(c * step_rows, (c + 1) * step_rows)
        value = dot_t(dq_ref[part, :], wq_ref[span, :])
        value = value + dot_t(dkv_now[part, :HEAD_WIDTH], wk_ref[span, :])
        return value + dot_t(dkv_now[part, HEAD_WIDTH:], wv_ref[span, :])

    def to_pair(k, c):
        return pltpu.make_async_remote_copy(
            src_ref=pair_out.at[k, c],
            dst_ref=pair_in.at[k, c],
            send_sem=pair_send.at[k, c],
            recv_sem=pair_recv.at[k, c],
            device_id={"tp": partner},
            device_id_type=MESH_ID,
        )

    def to_far(k, c):
        return pltpu.make_async_remote_copy(
            src_ref=far_out.at[k - 1, c],
            dst_ref=far_in.at[k - 1, c],
            send_sem=far_send.at[k - 1, c],
            recv_sem=far_recv.at[k - 1, c],
            device_id={"tp": peer_of(k)},
            device_id_type=MESH_ID,
        )

    def give(k, c):
        pair_out[k, c] = term(owner_of(k, False), c).astype(jnp.bfloat16)
        to_pair(k, c).start()

    def take(k, c):
        value = term(owner_of(k, True), c)
        to_pair(k, c).wait_recv()
        value = value + pair_in[k, c].astype(jnp.float32)
        if k == 0:
            near_sum[c] = value
        else:
            far_out[k - 1, c] = value.astype(jnp.bfloat16)
            to_far(k, c).start()

    order = [(k, c) for k in list(range(1, pairs)) + [0] for c in range(chunks)]
    give(*order[0])
    for n, item in enumerate(order):
        if n + 1 < len(order):
            give(*order[n + 1])
        take(*item)
        if n + 1 == (pairs - 1) * chunks:
            for d in range(reach - 1, 0, -1):
                send_on(d, 0)
    @pl.when(has_next)
    def _():
        for c in (1, 0):
            backward(1, c).wait_recv()
            dkv_ref[:, c * HEAD_WIDTH : (c + 1) * HEAD_WIDTH] = (
                scaled(0, c) + ret_in[0, c].astype(jnp.float32)
            ).astype(jnp.bfloat16)
        gather(0, 1).start()
        for k in range(1, pairs):
            gather(k, 0).start()

    def add_terms(pairs_of):
        for c in range(chunks):
            part = slice(c * step_rows, (c + 1) * step_rows)
            value = near_sum[c]
            for grads, wk, wv in pairs_of:
                value = value + dot_t(grads[part, :HEAD_WIDTH], wk[...])
                value = value + dot_t(grads[part, HEAD_WIDTH:], wv[...])
            near_sum[c] = value

    @pl.when(has_next)
    def _():
        for k, m in others:
            for c in range(2):
                fetch(k, m, c).wait_recv()
        own = span_of(place)
        add_terms([(dkv_ref, wk_ref.at[own], wv_ref.at[own])])
        gather(0, 1).wait_recv()
        add_terms([(dkv_all.at[0, 1], wk_all.at[0, 1], wv_all.at[0, 1])])
        for k in range(1, pairs):
            gather(k, 0).wait_recv()
            gather(k, 1).start()
            add_terms([(dkv_all.at[k, 0], wk_all.at[k, 0], wv_all.at[k, 0])])
        for k in range(1, pairs):
            gather(k, 1).wait_recv()
            add_terms([(dkv_all.at[k, 1], wk_all.at[k, 1], wv_all.at[k, 1])])
        for k, m in others:
            gather(k, m).wait_send()
            for c in range(2):
                fetch(k, m, c).wait_send()

    for c in range(chunks):
        value = near_sum[c]
        for k in range(1, pairs):
            to_far(k, c).wait_recv()
            value = value + far_in[k - 1, c].astype(jnp.float32)
        out_ref[c * step_rows : (c + 1) * step_rows, :] = value.astype(jnp.bfloat16)
    for k, c in order:
        to_pair(k, c).wait_send()
        if k > 0:
            to_far(k, c).wait_send()

    for d in range(reach):

        @pl.when((me >= d) & has_next)
        def _():
            for c in range(2):
                forward(d, c).wait_send()

        @pl.when(me >= d + 1)
        def _():
            for c in range(2):
                backward(d + 1, c).wait_send()


def body(
    query,
    key_head_rows,
    value_head_rows,
    output_gradient,
    doc_blocks,
    w_query,
    key_weight,
    value_weight,
):
    shards = lax.axis_size("seq")
    places = lax.axis_size("tp")
    pairs = places // 2
    reach = min(8, shards - 1)
    rows, q_width = query.shape
    nb = rows // BLOCK_POSITIONS
    cols = w_query.shape[0] // places
    width = (q_width // HEAD_WIDTH) * BLOCK_POSITIONS
    half, full = jnp.bfloat16, jnp.float32
    vmem = pl.BlockSpec(memory_space=pltpu.VMEM)
    anywhere = pl.BlockSpec(memory_space=pl.ANY)
    dma = pltpu.SemaphoreType.DMA
    return pl.pallas_call(
        functools.partial(attention_kernel, shards, reach, places),
        out_shape=jax.ShapeDtypeStruct((rows, cols), half),
        in_specs=[vmem] * 4 + [pl.BlockSpec(memory_space=pltpu.SMEM)] + [anywhere] * 3,
        out_specs=vmem,
        scratch_shapes=[
            pltpu.VMEM((rows, q_width), half),
            pltpu.VMEM((rows, 2 * HEAD_WIDTH), half),
            pltpu.VMEM((rows, 2 * HEAD_WIDTH), half),
            pltpu.VMEM((pairs, 2, rows, 2 * HEAD_WIDTH), half),
            pltpu.VMEM((pairs, 2, cols, HEAD_WIDTH), half),
            pltpu.VMEM((pairs, 2, cols, HEAD_WIDTH), half),
            pltpu.VMEM(w_query.shape, half),
            pltpu.VMEM(key_weight.shape, half),
            pltpu.VMEM(value_weight.shape, half),
            pltpu.VMEM((nb, rows // nb, cols), full),
            pltpu.VMEM((pairs, nb, rows // nb, cols), half),
            pltpu.VMEM((pairs, nb, rows // nb, cols), half),
            pltpu.VMEM((pairs - 1, nb, rows // nb, cols), half),
            pltpu.VMEM((pairs - 1, nb, rows // nb, cols), half),
            dma((3,)),
            dma((pairs, nb)),
            dma((pairs, nb)),
            dma((pairs - 1, nb)),
            dma((pairs - 1, nb)),
            dma((pairs, 2, 2)),
            dma((pairs, 2, 2)),
            dma((pairs, 2)),
            dma((pairs, 2)),
            pltpu.VMEM((reach, 2, rows, HEAD_WIDTH), half),
            pltpu.VMEM((nb, width, HEAD_WIDTH), half),
            pltpu.VMEM((nb, width, HEAD_WIDTH), half),
            pltpu.VMEM((nb, 8, width), full),
            pltpu.VMEM((nb, HEAD_WIDTH, width), full),
            pltpu.VMEM((reach + 1, nb, rows, width), half),
            pltpu.VMEM((reach + 1, 2, rows, HEAD_WIDTH), full),
            pltpu.VMEM((reach, 2, rows, HEAD_WIDTH), half),
            pltpu.VMEM((reach, 2, rows, HEAD_WIDTH), half),
            dma((reach, 2)),
            dma((reach, 2)),
            dma((reach, 2)),
            dma((reach, 2)),
        ],
        compiler_params=pltpu.CompilerParams(
            collective_id=0, has_side_effects=True, vmem_limit_bytes=60 * 1024 * 1024
        ),
        name="attention",
    )(
        query,
        key_head_rows,
        value_head_rows,
        output_gradient,
        doc_blocks,
        w_query,
        key_weight,
        value_weight,
    )


def solution(mesh):
    in_specs = (
        P(("groups", "seq"), "tp"),
        P(("groups", "seq"), "tp"),
        P(("groups", "seq"), "tp"),
        P(("groups", "seq"), "tp"),
        P(("groups", "seq"), None),
        P(None, "tp"),
        P(None, "tp"),
        P(None, "tp"),
    )
    out_specs = P(("groups", "seq"), "tp")
    return jax.shard_map(body, mesh=mesh, in_specs=in_specs, out_specs=out_specs, check_vma=False)
```
